256 devices in a mesh: section: 4 (over x), shard: 64 (over z, y, core).
Axes of the slice: x: 4, y: 4, z: 8, core: 2. Of those that a mesh axis runs over, the one named last changes fastest.
Arguments:
- features: bfloat16 [4096, 768], P('shard'), may hold values from -6 to 6
- tile_cols: int32 [4, 32, 16], P('section'), may hold values from 0 to 31
- live_tiles: int32 [4, 32], P('section'), may hold values from 1 to 16, 256 in all within a row
- tile_values: bfloat16 [4, 4096, 16, 128], P('section', 'shard'), may hold values from -0.375 to 0.375
- degrees: int32 [4, 4096], P('section', 'shard'), may hold values from 1 to 8
Outputs:
- hops: bfloat16 [4, 4096, 768], P('section', 'shard')
The draws below stay inside these ranges and needn't reach their ends.
Inputs may be any that keep to these rules, and one draw needn't show every extreme that they name: `live_tiles`: every row block has at least one live tile slot; the live counts of one relation sum to 256.
All inputs are finite; a program needn't handle non-finite values.
Results may differ from the reference program's by a relative error of at most 0.0056.
Values may be sent and summed in bfloat16 or wider, within the bound.
A program may use at most 64 MiB of HBM per device.

```python
import math
import jax
import jax.numpy as jnp
import numpy as np
from jax import lax

D = 768
TILE = 128
K = 16
NODES = 4096
ROW_BLOCKS = 32
N_SECTION = 4


def with_ends(drawn, stream_key, low, top_value):
    extent = drawn.shape
    spot = [jax.random.randint(jax.random.fold_in(stream_key, axis), (), 0, extent[axis]) for axis in range(len(extent))]
    drawn = drawn.at[tuple(spot)].set(low)
    longest = extent.index(max(extent))
    spot[longest] = (spot[longest] + 1) % extent[longest]
    return drawn.at[tuple(spot)].set(top_value)


def levels(rng, extent, split, least, largest):
    loudness, own = 1.0, jax.random.fold_in(rng, 6)
    for axis_at, shards_of in split:
        heights = jnp.exp(jax.random.uniform(jax.random.fold_in(own, axis_at), (shards_of,), jnp.float32, least / len(split), largest / len(split)))
        loudness = loudness * jnp.repeat(heights, extent[axis_at] // shards_of).reshape([-1 if axis == axis_at else 1 for axis in range(len(extent))])
    return loudness


def profile(amount, total, limit, lean):
    loads = [(1 << 20) // math.isqrt(grade ** lean) + 1 for grade in range(2, amount + 1)]
    surplus, given = total - limit - (amount - 1), [1] * (amount - 1)
    while surplus > 0:
        free = [i for i in range(amount - 1) if given[i] < limit]
        mass, budget = sum([loads[i] for i in free]), surplus
        for i in free:
            addition = min(limit - given[i], max(1, budget * loads[i] // mass), surplus)
            given[i] = given[i] + addition
            surplus = surplus - addition
    return np.array([limit] + given)


def ragged_sizes(own_key, count, total, bound, skew):
    if count == 2:
        one = jax.random.randint(own_key, (), max(1, total - bound), min(bound, total - 1) + 1)
        return jnp.stack([one, total - one])
    sizes = jnp.asarray(profile(count, total, bound, skew), jnp.int32)
    pairs = (count - 1) // 2
    giver, taker = sizes[1:1 + 2 * pairs:2], sizes[2:2 + 2 * pairs:2]
    room = jnp.minimum(giver - 1, bound - taker)
    moved = jax.random.randint(jax.random.fold_in(own_key, 1), (pairs,), 0, 1 << 20) % (room + 1)
    sizes = sizes.at[1:1 + 2 * pairs:2].set(giver - moved).at[2:2 + 2 * pairs:2].set(taker + moved)
    return sizes[jax.random.permutation(jax.random.fold_in(own_key, 2), count)]


def noise(stream_key, shape, width, bound, pieces=(), held_as=jnp.bfloat16):
    values = width * jax.random.normal(stream_key, shape, jnp.float32)
    if pieces:
        values = values * levels(stream_key, shape, pieces, -0.22, 0.18)
    return jnp.clip(values, -bound, bound).astype(held_as)


def setup_inputs(seed: int = 0) -> dict:
    key_list = jax.random.split(jax.random.key(seed), 6)
    features = noise(key_list[0], (NODES, D), 1.0, 6.0, ((0, 64),))
    tile_cols = with_ends(jax.random.randint(key_list[1], (N_SECTION, ROW_BLOCKS, K), 0, ROW_BLOCKS), jax.random.fold_in(key_list[1], 1), 0, ROW_BLOCKS - 1).astype(jnp.int32)
    live_tiles = jax.vmap(lambda own: ragged_sizes(own, ROW_BLOCKS, ROW_BLOCKS * K // 2, K, 2))(jax.random.split(key_list[2], N_SECTION)).reshape((N_SECTION, ROW_BLOCKS)).astype(jnp.int32)
    tile_values = noise(key_list[3], (N_SECTION, NODES, K, TILE), (K * TILE // 8) ** -0.5, 0.375, ((0, 4), (1, 64)))
    degrees = with_ends(jax.random.randint(key_list[4], (N_SECTION, NODES), 1, 9), jax.random.fold_in(key_list[4], 1), 1, 8).astype(jnp.int32)
    return {"features": features, "tile_cols": tile_cols, "live_tiles": live_tiles, "tile_values": tile_values, "degrees": degrees}


def reference(features, tile_cols, live_tiles, tile_values, degrees):
    previous = features
    collected = []
    for section in range(N_SECTION):
        blocks = previous.reshape(ROW_BLOCKS, TILE, D)

        def one_block(block_row):
            block_ids = tile_cols[section, block_row]
            source = blocks[block_ids].astype(jnp.float32)
            tile_rows = lax.dynamic_slice_in_dim(tile_values[section], block_row * TILE, TILE, 0).astype(jnp.float32)
            live_mask = (jnp.arange(K, dtype=jnp.int32) < live_tiles[section, block_row]).astype(jnp.float32)
            return jnp.einsum('rkc,kcd->rd', tile_rows * live_mask[None, :, None], source)
        summed = lax.map(one_block, jnp.arange(ROW_BLOCKS, dtype=jnp.int32)).reshape(NODES, D)
        row_scale = lax.rsqrt(degrees[section].astype(jnp.float32))
        previous = (summed * row_scale[:, None]).astype(jnp.bfloat16)
        collected.append(previous)
    return jnp.stack(collected)
```

```python
import jax
import jax.numpy as jnp
from jax import lax
from jax.experimental import pallas as pl
from jax.experimental.pallas import tpu as pltpu
from jax.sharding import PartitionSpec as P

MESH = pl.DeviceIdType.MESH
X, Y, Z = 4, 4, 8
HOPS = 4
TILE = 128
SLOTS = 16
COLS = 96
BLOCKS = Y * Z
HALF = 64
CHUNK = 16
SEND_UP = (0, 1, 2, 3)


def kernel(ft, a_in, meta, out, xg0, xg1, xg2, xg3, a_all, lhs, ybuf, half_x, mbuf, obuf, tbuf, sm,
           r_sem, s_sem, a_sem, c_sem, as_sem, m_sem, ms_sem, o_sem, os_sem, h_sem, l_sem):
    x = lax.axis_index("section")
    sh = lax.axis_index("shard")
    z, y, c = sh // 8, (sh // 2) % 4, sh % 2
    g = 2 * x + c
    xgs = (xg0, xg1, xg2, xg3)

    def at(dx=0, dy=0, dz=0, core=None):
        core = c if core is None else core
        return ((x + dx) % X, ((z + dz) % Z) * 8 + ((y + dy) % Y) * 2 + core)

    def blk(dy=0, dz=0):
        return ((y + dy) % Y) * Z + (z + dz) % Z

    def rows(core, first=0, count=HALF):
        return pl.ds(pl.multiple_of(core * HALF + first, 16), count)

    def send(src, dst, ssem, rsem, to):
        pltpu.make_async_remote_copy(src_ref=src, dst_ref=dst, send_sem=ssem, recv_sem=rsem,
                                     device_id=to, device_id_type=MESH).start()

    def arrived(ref, sem):
        pltpu.make_async_copy(ref, ref, sem).wait()

    other = 1 - c
    line = [(dx, same) for dx in range(X) for same in (True, False) if (dx, same) != (0, True)]

    barrier = pltpu.get_barrier_semaphore()
    peers = [at(dz=d) for d in range(1, Z)] + [at(dy=1), at(dy=-1)]
    peers += [at(dx=dx, core=c if same else other) for dx, same in line]
    for to in peers:
        pl.semaphore_signal(barrier, inc=1, device_id=to, device_id_type=MESH)
    pl.semaphore_wait(barrier, len(peers))

    sib = at(core=other)
    send(ft.at[other], half_x, h_sem.at[0], h_sem.at[1], sib)

    for q in range(4):
        for dx, k in ((1, q), (-1, 3 - q)):
            send(a_in.at[pl.ds(k * CHUNK, CHUNK)], a_all.at[x, rows(c, k * CHUNK, CHUNK)],
                 as_sem.at[0], a_sem.at[x, k], at(dx=dx))
    send(a_in, a_all.at[x, rows(c)], as_sem.at[2], c_sem.at[x], sib)
    own_a = pltpu.make_async_copy(a_in, a_all.at[x, rows(c)], l_sem.at[0])
    own_a.start()
    for dx, same in line:
        send(meta, mbuf.at[g], ms_sem.at[0], m_sem.at[g], at(dx=dx, core=c if same else other))
    mbuf[g] = meta[...]

    arrived(half_x, h_sem.at[1])
    xg0[blk()] = (ft[c].astype(jnp.float32) + half_x[...].astype(jnp.float32)).astype(jnp.bfloat16)

    def relay(h, dz):
        xg = xgs[h]
        if dz in SEND_UP:
            b, to = blk(-1, dz), at(dy=1)
        else:
            b, to = blk(1, dz), at(dy=-1)
        arrived(xg.at[b], r_sem.at[h, b])
        send(xg.at[b], xg.at[b], s_sem.at[h], r_sem.at[h, b], to)

    def spread(h, dz):
        xg = xgs[h]
        b = blk(0, dz)
        arrived(xg.at[b], r_sem.at[h, b])
        for dy in (1, -1):
            send(xg.at[b], xg.at[b], s_sem.at[h], r_sem.at[h, b], at(dy=dy))

    def gather_start(h, src):
        b = blk()
        for dz in (4, 3, -3, 2, -2, 1, -1):
            send(src, xgs[h].at[b], s_sem.at[h], r_sem.at[h, b], at(dz=dz))
        for dy in (1, -1):
            send(src, xgs[h].at[b], s_sem.at[h], r_sem.at[h, b], at(dy=dy))

    def gather_rest(h):
        relay(h, 0)
        spread(h, 1)
        spread(h, -1)
        spread(h, 2)
        spread(h, -2)
        relay(h, 1)
        relay(h, -1)
        spread(h, 3)
        spread(h, -3)
        relay(h, 2)
        relay(h, -2)
        spread(h, 4)
        relay(h, 3)
        relay(h, -3)
        relay(h, 4)
        for dz in (0, 1, -1, 2, -2, 3, -3, 4):
            b = blk(1 if dz in SEND_UP else -1, dz)
            arrived(xgs[h].at[b], r_sem.at[h, b])
        for dz in (0, 1, -1, 2, -2, 3, -3, 4):
            b = blk(2, dz)
            arrived(xgs[h].at[b], r_sem.at[h, b])

    def tile_chunk(s, k):
        ref = a_all.at[s, rows(c, k * CHUNK, CHUNK)]
        arrived(ref, a_sem.at[s, k])
        return ref

    def compute(h):
        for k in range(SLOTS):
            lhs[:, k * TILE:(k + 1) * TILE] = xgs[h][sm[2 * h, 1, k]]
        acc = lax.dot_general(lhs[...], a_all[h], (((1,), (1,)), ((), ())),
                              preferred_element_type=jnp.float32)
        degree = mbuf[2 * h, 0:1, :] + mbuf[2 * h + 1, 0:1, :]
        val = (acc * lax.rsqrt(degree.astype(jnp.float32))).astype(jnp.bfloat16)
        ybuf[h] = val
        if h < HOPS - 1:
            xgs[h + 1][blk()] = val
            gather_start(h + 1, ybuf.at[h])

        @pl.when(x == h)
        def _():
            obuf[g] = ybuf[h]
            send(ybuf.at[h], obuf.at[g], os_sem.at[0], o_sem.at[g], sib)

        @pl.when(x != h)
        def _():
            for core in (0, 1):
                send(ybuf.at[h], obuf.at[g], os_sem.at[0], o_sem.at[g], (h, (sh // 2) * 2 + core))

    gather_start(0, xg0.at[blk()])

    left, right, far = (x - 1) % X, (x + 1) % X, (x + 2) % X
    for q in range(2):
        for s, k, dx in ((left, q, 1), (right, 3 - q, -1)):
            ref = tile_chunk(s, k)
            send(ref, ref, as_sem.at[1], a_sem.at[s, k], at(dx=dx))
    gather_rest(0)
    for dx, same in line:
        p = 2 * ((x + dx) % X) + (c if same else other)
        arrived(mbuf.at[p], m_sem.at[p])
    to_sm = pltpu.make_async_copy(mbuf, sm, l_sem.at[1])
    to_sm.start()
    for s, ks in ((left, (2, 3)), (right, (1, 0)), (far, (0, 1, 2, 3))):
        for k in ks:
            tile_chunk(s, k)
        piece = a_all.at[s, rows(c)]
        send(piece, piece, as_sem.at[2], c_sem.at[s], sib)
    own_a.wait()
    for s in range(X):
        arrived(a_all.at[s, rows(other)], c_sem.at[s])
    to_sm.wait()
    compute(0)
    for h in range(1, HOPS):
        gather_rest(h)
        compute(h)

    for dx, same in line:
        p = 2 * ((x + dx) % X) + (c if same else other)
        arrived(obuf.at[p], o_sem.at[p])
    for i in range(8):
        tbuf[:, i * COLS:(i + 1) * COLS] = obuf[i].astype(jnp.float32).T
    out[...] = tbuf[pl.ds(pl.multiple_of(c * HALF, HALF), HALF), :].astype(jnp.bfloat16)

    arrived(half_x, h_sem.at[0])
    arrived(a_all.at[0], as_sem.at[0])
    arrived(a_all.at[0, pl.ds(0, HALF)], as_sem.at[1])
    arrived(a_all.at[pl.ds(0, 2)], as_sem.at[2])
    arrived(mbuf.at[pl.ds(0, 7)], ms_sem.at[0])
    arrived(obuf.at[pl.ds(0, 7)], os_sem.at[0])
    for h in range(HOPS):
        arrived(xgs[h].at[pl.ds(0, 31)], s_sem.at[h])


def per_device(features, tile_cols, live_tiles, tile_values, degrees):
    x = lax.axis_index("section")
    sh = lax.axis_index("shard")
    c = sh % 2
    row = sh // 2
    part = lax.dynamic_slice(features, (0, 2 * COLS * x), (HALF, 2 * COLS)).T
    zero = jnp.zeros_like(part)
    part = jnp.where(c == 0, jnp.concatenate([part, zero], 1), jnp.concatenate([zero, part], 1))
    ft = part.reshape(2, COLS, TILE)
    live = lax.dynamic_index_in_dim(live_tiles[0], row, 0, keepdims=False)
    mask = jnp.arange(SLOTS, dtype=jnp.int32) < live
    a_in = jnp.where(mask[None, :, None], tile_values[0], 0).reshape(HALF, SLOTS * TILE)
    cols = lax.dynamic_index_in_dim(tile_cols[0], row, 0, keepdims=False)
    cols = (cols % Y) * Z + cols // Y
    d = degrees[0]
    dz = jnp.zeros_like(d)
    d = jnp.where(c == 0, jnp.concatenate([d, dz]), jnp.concatenate([dz, d]))
    meta = jnp.concatenate([d[None], jnp.pad(cols, (0, TILE - SLOTS))[None],
                            jnp.zeros((6, TILE), jnp.int32)], 0)
    vm = pl.BlockSpec(memory_space=pltpu.VMEM)
    dma = pltpu.SemaphoreType.DMA
    slab = pltpu.VMEM((BLOCKS, COLS, TILE), jnp.bfloat16)
    res = pl.pallas_call(
        kernel,
        out_shape=jax.ShapeDtypeStruct((HALF, 8 * COLS), jnp.bfloat16),
        in_specs=[vm] * 3,
        out_specs=vm,
        scratch_shapes=[
            slab, slab, slab, slab,
            pltpu.VMEM((X, TILE, SLOTS * TILE), jnp.bfloat16),
            pltpu.VMEM((COLS, SLOTS * TILE), jnp.bfloat16),
            pltpu.VMEM((HOPS, COLS, TILE), jnp.bfloat16),
            pltpu.VMEM((COLS, TILE), jnp.bfloat16),
            pltpu.VMEM((8, 8, TILE), jnp.int32),
            pltpu.VMEM((8, COLS, TILE), jnp.bfloat16),
            pltpu.VMEM((TILE, 8 * COLS), jnp.float32),
            pltpu.SMEM((8, 8, TILE), jnp.int32),
            dma((HOPS, BLOCKS)), dma((HOPS,)), dma((X, 4)), dma((X,)), dma((3,)),
            dma((8,)), dma((1,)), dma((8,)), dma((1,)), dma((2,)), dma((2,)),
        ],
        compiler_params=pltpu.CompilerParams(collective_id=0, has_side_effects=True,
                                             vmem_limit_bytes=40 * 1024 * 1024),
        name="propagate",
    )(ft, a_in, meta)
    return res[None]


def solution(mesh):
    in_specs = (
        P("shard", None),
        P("section", None, None),
        P("section", None),
        P("section", "shard", None, None),
        P("section", "shard"),
    )
    return jax.shard_map(per_device, mesh=mesh, in_specs=in_specs,
                         out_specs=P("section", "shard", None), check_vma=False)
```

```python
import jax
import jax.numpy as jnp
from jax import lax
from jax.experimental import pallas as pl
from jax.experimental.pallas import tpu as pltpu
from jax.sharding import PartitionSpec as P

MESH = pl.DeviceIdType.MESH
X, Y, Z = 4, 4, 8
HOPS = 4
TILE = 128
SLOTS = 16
COLS = 96
BLOCKS = Y * Z
HALF = 64
CHUNK = 16
DYS = (0, 1, -1, 2)
DZS = (0, 1, -1, 2, -2, 3, -3, 4)
COLS_AT = 8


def parent(dy, dz):
    if dy == 0 or dz == 0:
        return (0, 0)
    if abs(dz) == 1 or (abs(dz) == 2 and dy != 2):
        return (dy, 0)
    return (0, dz)


def far(o):
    return abs(o[0]) + abs(o[1])


OFFSETS = [(dy, dz) for dz in DZS for dy in DYS if dy or dz]
KIDS = {}
for _o in sorted(OFFSETS, key=lambda o: -far(o)):
    KIDS.setdefault(parent(*_o), []).append(_o)
DIRECT = sorted(KIDS.pop((0, 0)), key=lambda o: (o not in KIDS, -far(o)))
RELAYS = sorted(KIDS, key=far)
LEAVES = [o for o in sorted(OFFSETS, key=lambda o: (far(o) + far(parent(*o)), far(o))) if o not in KIDS]


def kernel(feat, cols, live, deg, a_in, out, xg0, xg1, xg2, xg3, a_all, lhs, ybuf, half_x, fpad, ft, meta, mbuf, obuf, sm,
           r_sem, s_sem, a_sem, c_sem, as_sem, m_sem, ms_sem, o_sem, os_sem, h_sem, l_sem):
    x = lax.axis_index("section")
    sh = lax.axis_index("shard")
    z, y, c = sh // 8, (sh // 2) % 4, sh % 2
    g = 2 * x + c
    xgs = (xg0, xg1, xg2, xg3)

    def at(dx=0, dy=0, dz=0, core=None):
        core = c if core is None else core
        return ((x + dx) % X, ((z + dz) % Z) * 8 + ((y + dy) % Y) * 2 + core)

    def blk(dy=0, dz=0):
        return ((y + dy) % Y) * Z + (z + dz) % Z

    def rows(core, first=0, count=HALF):
        return pl.ds(pl.multiple_of(core * HALF + first, 16), count)

    def cols_of(group):
        return pl.ds(pl.multiple_of(group * COLS, 16), COLS)

    def send(src, dst, ssem, rsem, to):
        pltpu.make_async_remote_copy(src_ref=src, dst_ref=dst, send_sem=ssem, recv_sem=rsem,
                                     device_id=to, device_id_type=MESH).start()

    def arrived(ref, sem):
        pltpu.make_async_copy(ref, ref, sem).wait()

    other = 1 - c
    line = [(dx, same) for dx in range(X) for same in (True, False) if (dx, same) != (0, True)]

    barrier = pltpu.get_barrier_semaphore()
    peers = [at(dz=d) for d in range(1, Z)] + [at(dy=d) for d in range(1, Y)]
    peers += [at(dx=dx, core=c if same else other) for dx, same in line]
    for to in peers:
        pl.semaphore_signal(barrier, inc=1, device_id=to, device_id_type=MESH)

    fpad[...] = jnp.zeros_like(fpad)
    fpad[rows(c), :] = feat[...].astype(jnp.float32)
    ft[...] = fpad[...].T.astype(jnp.bfloat16)
    lane = lax.broadcasted_iota(jnp.int32, (SLOTS, BLOCKS), 1)
    col = jnp.sum(jnp.where(lane == sh // 2, cols[0], 0), axis=1, keepdims=True)
    col = (col & (Y - 1)) * Z + (col >> 2)
    meta[pl.ds(COLS_AT, SLOTS), :] = jnp.broadcast_to(col, (SLOTS, TILE))
    count = jnp.sum(jnp.where(lane[0:1] == sh // 2, live[...], 0), axis=1, keepdims=True)
    d = deg[...]
    none = jnp.zeros_like(d)
    meta[0:1, :] = jnp.where(c == 0, jnp.concatenate([d, none], 1), jnp.concatenate([none, d], 1))
    meta[1:2, :] = jnp.broadcast_to(count, (1, TILE))
    pl.semaphore_wait(barrier, len(peers))

    sib = at(core=other)
    send(ft.at[cols_of(2 * x + other)], half_x, h_sem.at[0], h_sem.at[1], sib)

    for q in range(4):
        for dx, k in ((1, q), (-1, 3 - q)):
            send(a_in.at[pl.ds(k * CHUNK, CHUNK)], a_all.at[x, rows(c, k * CHUNK, CHUNK)],
                 as_sem.at[0], a_sem.at[x, k], at(dx=dx))
    send(a_in, a_all.at[x, rows(c)], as_sem.at[2], c_sem.at[x], sib)
    own_a = pltpu.make_async_copy(a_in, a_all.at[x, rows(c)], l_sem.at[0])
    own_a.start()
    for dx, same in line:
        send(meta, mbuf.at[g], ms_sem.at[0], m_sem.at[g], at(dx=dx, core=c if same else other))
    mbuf[g] = meta[...]

    arrived(half_x, h_sem.at[1])
    xg0[blk()] = (ft[cols_of(g), :].astype(jnp.float32) + half_x[...].astype(jnp.float32)).astype(jnp.bfloat16)

    def gather_start(h, src):
        b = blk()
        for dy, dz in DIRECT:
            send(src, xgs[h].at[b], s_sem.at[h], r_sem.at[h, b], at(dy=dy, dz=dz))

    def gather_relay(h):
        for o in RELAYS:
            b = blk(-o[0], -o[1])
            ref = xgs[h].at[b]
            arrived(ref, r_sem.at[h, b])
            for k in KIDS[o]:
                send(ref, ref, s_sem.at[h], r_sem.at[h, b], at(dy=k[0] - o[0], dz=k[1] - o[1]))

    def gather_rest(h):
        for o in LEAVES:
            b = blk(-o[0], -o[1])
            arrived(xgs[h].at[b], r_sem.at[h, b])

    def tile_chunk(s, k):
        ref = a_all.at[s, rows(c, k * CHUNK, CHUNK)]
        arrived(ref, a_sem.at[s, k])
        return ref

    def compute(h):
        for k in range(SLOTS):
            on = (mbuf[2 * h, 1:2, :] > k).astype(jnp.float32).astype(jnp.bfloat16)
            lhs[:, k * TILE:(k + 1) * TILE] = xgs[h][sm[h, k, 0]] * on
        acc = lax.dot_general(lhs[...], a_all[h], (((1,), (1,)), ((), ())),
                              preferred_element_type=jnp.float32)
        degree = mbuf[2 * h, 0:1, :] + mbuf[2 * h + 1, 0:1, :]
        val = (acc * lax.rsqrt(degree.astype(jnp.float32))).astype(jnp.bfloat16)
        ybuf[h] = val
        if h < HOPS - 1:
            xgs[h + 1][blk()] = val
            gather_start(h + 1, ybuf.at[h])

        @pl.when(x == h)
        def _():
            obuf[g] = ybuf[h]
            send(ybuf.at[h], obuf.at[g], os_sem.at[0], o_sem.at[g], sib)

        @pl.when(x != h)
        def _():
            for core in (0, 1):
                send(ybuf.at[h], obuf.at[g], os_sem.at[0], o_sem.at[g], (h, (sh // 2) * 2 + core))

    gather_start(0, xg0.at[blk()])
    gather_relay(0)

    left, right, far = (x - 1) % X, (x + 1) % X, (x + 2) % X
    for q in range(2):
        for s, k, dx in ((left, q, 1), (right, 3 - q, -1)):
            ref = tile_chunk(s, k)
            send(ref, ref, as_sem.at[1], a_sem.at[s, k], at(dx=dx))
    gather_rest(0)
    for dx, same in line:
        p = 2 * ((x + dx) % X) + (c if same else other)
        arrived(mbuf.at[p], m_sem.at[p])
    to_sm = [pltpu.make_async_copy(mbuf.at[2 * s, pl.ds(COLS_AT, SLOTS)], sm.at[s], l_sem.at[1 + s]) for s in range(X)]
    for copy in to_sm:
        copy.start()
    for s, ks in ((left, (2, 3)), (right, (1, 0)), (far, (0, 1, 2, 3))):
        for k in ks:
            tile_chunk(s, k)
        piece = a_all.at[s, rows(c)]
        send(piece, piece, as_sem.at[2], c_sem.at[s], sib)
    own_a.wait()
    for s in range(X):
        arrived(a_all.at[s, rows(other)], c_sem.at[s])
    for copy in to_sm:
        copy.wait()
    compute(0)
    for h in range(1, HOPS):
        gather_relay(h)
        gather_rest(h)
        compute(h)

    for dx, same in line:
        p = 2 * ((x + dx) % X) + (c if same else other)
        arrived(obuf.at[p], o_sem.at[p])
    full = obuf[...].reshape(8 * COLS, TILE).astype(jnp.float32).T
    out[...] = jnp.where(c == 0, full[:HALF], full[HALF:]).astype(jnp.bfloat16)

    arrived(half_x, h_sem.at[0])
    arrived(a_all.at[0], as_sem.at[0])
    arrived(a_all.at[0, pl.ds(0, HALF)], as_sem.at[1])
    arrived(a_all.at[pl.ds(0, 2)], as_sem.at[2])
    arrived(mbuf.at[pl.ds(0, 7)], ms_sem.at[0])
    arrived(obuf.at[pl.ds(0, 7)], os_sem.at[0])
    for h in range(HOPS):
        arrived(xgs[h].at[pl.ds(0, 31)], s_sem.at[h])


def per_device(features, tile_cols, live_tiles, tile_values, degrees):
    a_in = tile_values[0].reshape(HALF, SLOTS * TILE)
    cols = jnp.swapaxes(tile_cols, 1, 2)
    vm = pl.BlockSpec(memory_space=pltpu.VMEM)
    dma = pltpu.SemaphoreType.DMA
    slab = pltpu.VMEM((BLOCKS, COLS, TILE), jnp.bfloat16)
    res = pl.pallas_call(
        kernel,
        out_shape=jax.ShapeDtypeStruct((HALF, 8 * COLS), jnp.bfloat16),
        in_specs=[vm] * 5,
        out_specs=vm,
        scratch_shapes=[
            slab, slab, slab, slab,
            pltpu.VMEM((X, TILE, SLOTS * TILE), jnp.bfloat16),
            pltpu.VMEM((COLS, SLOTS * TILE), jnp.bfloat16),
            pltpu.VMEM((HOPS, COLS, TILE), jnp.bfloat16),
            pltpu.VMEM((COLS, TILE), jnp.bfloat16),
            pltpu.VMEM((TILE, 8 * COLS), jnp.float32),
            pltpu.VMEM((8 * COLS, TILE), jnp.bfloat16),
            pltpu.VMEM((24, TILE), jnp.int32),
            pltpu.VMEM((8, 24, TILE), jnp.int32),
            pltpu.VMEM((8, COLS, TILE), jnp.bfloat16),
            pltpu.SMEM((X, SLOTS, TILE), jnp.int32),
            dma((HOPS, BLOCKS)), dma((HOPS,)), dma((X, 4)), dma((X,)), dma((3,)),
            dma((8,)), dma((1,)), dma((8,)), dma((1,)), dma((2,)), dma((5,)),
        ],
        compiler_params=pltpu.CompilerParams(collective_id=0, has_side_effects=True,
                                             vmem_limit_bytes=40 * 1024 * 1024),
        name="propagate",
    )(features, cols, live_tiles, degrees, a_in)
    return res[None]


def solution(mesh):
    in_specs = (
        P("shard", None),
        P("section", None, None),
        P("section", None),
        P("section", "shard", None, None),
        P("section", "shard"),
    )
    return jax.shard_map(per_device, mesh=mesh, in_specs=in_specs,
                         out_specs=P("section", "shard", None), check_vma=False)
```

```python
import jax
import jax.numpy as jnp
from jax import lax
from jax.experimental import pallas as pl
from jax.experimental.pallas import tpu as pltpu
from jax.sharding import PartitionSpec as P

MESH = pl.DeviceIdType.MESH
X, Y, Z = 4, 4, 8
HOPS = 4
TILE = 128
SLOTS = 16
COLS = 96
BLOCKS = Y * Z
HALF = 64
CHUNK = 16
DYS = (0, 1, -1, 2)
DZS = (0, 1, -1, 2, -2, 3, -3, 4)
COLS_AT = 8


def parent(dy, dz):
    if dy == 0 or dz == 0:
        return (0, 0)
    if abs(dz) == 1 or (abs(dz) == 2 and dy != 2):
        return (dy, 0)
    return (0, dz)


def far(o):
    return abs(o[0]) + abs(o[1])


OFFSETS = [(dy, dz) for dz in DZS for dy in DYS if dy or dz]
KIDS = {}
for _o in sorted(OFFSETS, key=lambda o: -far(o)):
    KIDS.setdefault(parent(*_o), []).append(_o)
DIRECT = sorted(KIDS.pop((0, 0)), key=lambda o: (o not in KIDS, -far(o)))
RELAYS = sorted(KIDS, key=far)
LEAVES = [o for o in sorted(OFFSETS, key=lambda o: (far(o) + far(parent(*o)), far(o))) if o not in KIDS]


def kernel(feat, cols, live, deg, a_in, out, xg0, xg1, xg2, xg3, a_all, lhs, ybuf, half_x, fpad, ft, meta, mbuf, obuf, sm,
           r_sem, s_sem, a_sem, c_sem, as_sem, m_sem, ms_sem, o_sem, os_sem, h_sem, l_sem):
    x = lax.axis_index("section")
    sh = lax.axis_index("shard")
    z, y, c = sh // 8, (sh // 2) % 4, sh % 2
    g = 2 * x + c
    xgs = (xg0, xg1, xg2, xg3)

    def at(dx=0, dy=0, dz=0, core=None):
        core = c if core is None else core
        return ((x + dx) % X, ((z + dz) % Z) * 8 + ((y + dy) % Y) * 2 + core)

    def blk(dy=0, dz=0):
        return ((y + dy) % Y) * Z + (z + dz) % Z

    def rows(core, first=0, count=HALF):
        return pl.ds(pl.multiple_of(core * HALF + first, 16), count)

    def cols_of(group):
        return pl.ds(pl.multiple_of(group * COLS, 16), COLS)

    def send(src, dst, ssem, rsem, to):
        pltpu.make_async_remote_copy(src_ref=src, dst_ref=dst, send_sem=ssem, recv_sem=rsem,
                                     device_id=to, device_id_type=MESH).start()

    def arrived(ref, sem):
        pltpu.make_async_copy(ref, ref, sem).wait()

    other = 1 - c
    line = [(dx, same) for dx in range(X) for same in (True, False) if (dx, same) != (0, True)]

    barrier = pltpu.get_barrier_semaphore()
    peers = [at(dz=d) for d in range(1, Z)] + [at(dy=d) for d in range(1, Y)]
    peers += [at(dx=dx, core=c if same else other) for dx, same in line]
    for to in peers:
        pl.semaphore_signal(barrier, inc=1, device_id=to, device_id_type=MESH)

    fpad[...] = jnp.zeros_like(fpad)
    for i in range(X):
        @pl.when(x == i)
        def _():
            fpad[rows(c), :] = feat[:, 2 * COLS * i:2 * COLS * (i + 1)].astype(jnp.float32)
    ft[...] = fpad[...].T.astype(jnp.bfloat16)
    pl.semaphore_wait(barrier, len(peers))

    sib = at(core=other)
    send(ft.at[cols_of(other)], half_x, h_sem.at[0], h_sem.at[1], sib)

    for q in range(4):
        for dx, k in ((1, q), (-1, 3 - q)):
            send(a_in.at[pl.ds(k * CHUNK, CHUNK)], a_all.at[x, rows(c, k * CHUNK, CHUNK)],
                 as_sem.at[0], a_sem.at[x, k], at(dx=dx))
    send(a_in, a_all.at[x, rows(c)], as_sem.at[2], c_sem.at[x], sib)
    own_a = pltpu.make_async_copy(a_in, a_all.at[x, rows(c)], l_sem.at[0])
    own_a.start()
    def gather_start(h, src):
        b = blk()
        for dy, dz in DIRECT:
            send(src, xgs[h].at[b], s_sem.at[h], r_sem.at[h, b], at(dy=dy, dz=dz))

    def gather_relay(h):
        for o in RELAYS:
            b = blk(-o[0], -o[1])
            ref = xgs[h].at[b]
            arrived(ref, r_sem.at[h, b])
            for k in KIDS[o]:
                send(ref, ref, s_sem.at[h], r_sem.at[h, b], at(dy=k[0] - o[0], dz=k[1] - o[1]))

    def gather_rest(h):
        for o in LEAVES:
            b = blk(-o[0], -o[1])
            arrived(xgs[h].at[b], r_sem.at[h, b])

    def tile_chunk(s, k):
        ref = a_all.at[s, rows(c, k * CHUNK, CHUNK)]
        arrived(ref, a_sem.at[s, k])
        return ref

    def compute(h):
        for k in range(SLOTS):
            on = (mbuf[2 * h, 1:2, :] > k).astype(jnp.float32).astype(jnp.bfloat16)
            lhs[:, k * TILE:(k + 1) * TILE] = xgs[h][sm[h, k, 0]] * on
        acc = lax.dot_general(lhs[...], a_all[h], (((1,), (1,)), ((), ())),
                              preferred_element_type=jnp.float32)
        degree = mbuf[2 * h, 0:1, :] + mbuf[2 * h + 1, 0:1, :]
        val = (acc * lax.rsqrt(degree.astype(jnp.float32))).astype(jnp.bfloat16)
        ybuf[h] = val
        if h < HOPS - 1:
            xgs[h + 1][blk()] = val
            gather_start(h + 1, ybuf.at[h])

        @pl.when(x == h)
        def _():
            obuf[g] = ybuf[h]
            send(ybuf.at[h], obuf.at[g], os_sem.at[0], o_sem.at[g], sib)

        @pl.when(x != h)
        def _():
            for core in (0, 1):
                send(ybuf.at[h], obuf.at[g], os_sem.at[0], o_sem.at[g], (h, (sh // 2) * 2 + core))

    arrived(half_x, h_sem.at[1])
    xg0[blk()] = (ft[cols_of(c), :].astype(jnp.float32) + half_x[...].astype(jnp.float32)).astype(jnp.bfloat16)
    gather_start(0, xg0.at[blk()])
    lane = lax.broadcasted_iota(jnp.int32, (SLOTS, BLOCKS), 1)
    col = jnp.sum(jnp.where(lane == sh // 2, cols[0], 0), axis=1, keepdims=True)
    col = (col & (Y - 1)) * Z + (col >> 2)
    meta[pl.ds(COLS_AT, SLOTS), :] = jnp.broadcast_to(col, (SLOTS, TILE))
    count = jnp.sum(jnp.where(lane[0:1] == sh // 2, live[...], 0), axis=1, keepdims=True)
    d = deg[...]
    none = jnp.zeros_like(d)
    meta[0:1, :] = jnp.where(c == 0, jnp.concatenate([d, none], 1), jnp.concatenate([none, d], 1))
    meta[1:2, :] = jnp.broadcast_to(count, (1, TILE))
    for dx, same in line:
        send(meta, mbuf.at[g], ms_sem.at[0], m_sem.at[g], at(dx=dx, core=c if same else other))
    mbuf[g] = meta[...]
    gather_relay(0)

    left, right, far_x = (x - 1) % X, (x + 1) % X, (x + 2) % X
    for q in range(2):
        for s, k, dx in ((left, q, 1), (right, 3 - q, -1)):
            ref = tile_chunk(s, k)
            send(ref, ref, as_sem.at[1], a_sem.at[s, k], at(dx=dx))
    for s, ks in ((left, (2, 3)), (right, (1, 0)), (far_x, (0, 1, 2, 3))):
        for k in ks:
            tile_chunk(s, k)
        piece = a_all.at[s, rows(c)]
        send(piece, piece, as_sem.at[2], c_sem.at[s], sib)
    for dx, same in line:
        p = 2 * ((x + dx) % X) + (c if same else other)
        arrived(mbuf.at[p], m_sem.at[p])
    to_sm = [pltpu.make_async_copy(mbuf.at[2 * s, pl.ds(COLS_AT, SLOTS)], sm.at[s], l_sem.at[1 + s]) for s in range(X)]
    for copy in to_sm:
        copy.start()
    own_a.wait()
    for copy in to_sm:
        copy.wait()
    for h in range(HOPS):
        if h:
            gather_relay(h)
        gather_rest(h)
        arrived(a_all.at[h, rows(other)], c_sem.at[h])
        compute(h)

    for dx, same in line:
        p = 2 * ((x + dx) % X) + (c if same else other)
        arrived(obuf.at[p], o_sem.at[p])
    full = obuf[...].reshape(8 * COLS, TILE).astype(jnp.float32).T
    out[...] = jnp.where(c == 0, full[:HALF], full[HALF:]).astype(jnp.bfloat16)

    arrived(half_x, h_sem.at[0])
    arrived(a_all.at[0], as_sem.at[0])
    arrived(a_all.at[0, pl.ds(0, HALF)], as_sem.at[1])
    arrived(a_all.at[pl.ds(0, 2)], as_sem.at[2])
    arrived(mbuf.at[pl.ds(0, 7)], ms_sem.at[0])
    arrived(obuf.at[pl.ds(0, 7)], os_sem.at[0])
    for h in range(HOPS):
        arrived(xgs[h].at[pl.ds(0, 31)], s_sem.at[h])


def per_device(features, tile_cols, live_tiles, tile_values, degrees):
    a_in = tile_values[0].reshape(HALF, SLOTS * TILE)
    cols = jnp.swapaxes(tile_cols, 1, 2)
    vm = pl.BlockSpec(memory_space=pltpu.VMEM)
    dma = pltpu.SemaphoreType.DMA
    slab = pltpu.VMEM((BLOCKS, COLS, TILE), jnp.bfloat16)
    res = pl.pallas_call(
        kernel,
        out_shape=jax.ShapeDtypeStruct((HALF, 8 * COLS), jnp.bfloat16),
        in_specs=[vm] * 5,
        out_specs=vm,
        scratch_shapes=[
            slab, slab, slab, slab,
            pltpu.VMEM((X, TILE, SLOTS * TILE), jnp.bfloat16),
            pltpu.VMEM((COLS, SLOTS * TILE), jnp.bfloat16),
            pltpu.VMEM((HOPS, COLS, TILE), jnp.bfloat16),
            pltpu.VMEM((COLS, TILE), jnp.bfloat16),
            pltpu.VMEM((TILE, 2 * COLS), jnp.float32),
            pltpu.VMEM((2 * COLS, TILE), jnp.bfloat16),
            pltpu.VMEM((24, TILE), jnp.int32),
            pltpu.VMEM((8, 24, TILE), jnp.int32),
            pltpu.VMEM((8, COLS, TILE), jnp.bfloat16),
            pltpu.SMEM((X, SLOTS, TILE), jnp.int32),
            dma((HOPS, BLOCKS)), dma((HOPS,)), dma((X, 4)), dma((X,)), dma((3,)),
            dma((8,)), dma((1,)), dma((8,)), dma((1,)), dma((2,)), dma((5,)),
        ],
        compiler_params=pltpu.CompilerParams(collective_id=0, has_side_effects=True,
                                             vmem_limit_bytes=40 * 1024 * 1024),
        name="propagate",
    )(features, cols, live_tiles, degrees, a_in)
    return res[None]


def solution(mesh):
    in_specs = (
        P("shard", None),
        P("section", None, None),
        P("section", None),
        P("section", "shard", None, None),
        P("section", "shard"),
    )
    return jax.shard_map(per_device, mesh=mesh, in_specs=in_specs,
                         out_specs=P("section", "shard", None), check_vma=False)
```

```python
import jax
import jax.numpy as jnp
from jax import lax
from jax.experimental import pallas as pl
from jax.experimental.pallas import tpu as pltpu
from jax.sharding import PartitionSpec as P

MESH = pl.DeviceIdType.MESH
X, Y, Z = 4, 4, 8
HOPS = 4
TILE = 128
SLOTS = 16
BLOCKS = Y * Z
HALF = 64
CHUNK = 16
CHIP = 192
WIDTH = (64, 128)
FIRST = (0, 64)
COLS_AT = 8
DYS = (0, 1, -1, 2)
DZS = (0, 1, -1, 2, -2, 3, -3, 4)


def parent(dy, dz):
    if dy == 0 or dz == 0:
        return (0, 0)
    if abs(dz) <= 2:
        return (dy, 0)
    return (0, dz)


def far(o):
    return abs(o[0]) + abs(o[1])


OFFSETS = [(dy, dz) for dz in DZS for dy in DYS if dy or dz]
KIDS = {}
for _o in sorted(OFFSETS, key=lambda o: -far(o)):
    KIDS.setdefault(parent(*_o), []).append(_o)
DIRECT = sorted(KIDS.pop((0, 0)), key=lambda o: (o not in KIDS, -far(o)))
RELAYS = sorted(KIDS, key=far)
LEAVES = [o for o in sorted(OFFSETS, key=lambda o: (far(o) + far(parent(*o)), far(o))) if o not in KIDS]


def send(src, dst, ssem, rsem, to):
    pltpu.make_async_remote_copy(src_ref=src, dst_ref=dst, send_sem=ssem, recv_sem=rsem,
                                 device_id=to, device_id_type=MESH).start()


def arrived(ref, sem):
    pltpu.make_async_copy(ref, ref, sem).wait()


def kernel(*refs):
    core = lax.axis_index("shard") % 2
    for c in (0, 1):
        @pl.when(core == c)
        def _():
            run(c, *refs)


def run(c, feat, cols, live, deg, a_in, out, xg0, xg1, xg2, xg3, a_all, lhs, ybuf, tbuf, half_x, ft, meta, mbuf, obuf, sm,
        r_sem, s_sem, a_sem, c_sem, as_sem, m_sem, ms_sem, o_sem, os_sem, h_sem, l_sem):
    x = lax.axis_index("section")
    sh = lax.axis_index("shard")
    z, y = sh // 8, (sh // 2) % 4
    g = 2 * x + c
    xgs = (xg0, xg1, xg2, xg3)
    other = 1 - c
    w = WIDTH[c]
    mine, theirs = pl.ds(FIRST[c], w), pl.ds(FIRST[other], WIDTH[other])

    def at(dx=0, dy=0, dz=0, core=c):
        return ((x + dx) % X, ((z + dz) % Z) * 8 + ((y + dy) % Y) * 2 + core)

    def blk(dy=0, dz=0):
        return ((y + dy) % Y) * Z + (z + dz) % Z

    def block(h, b):
        return xgs[h].at[b, pl.ds(0, w)]

    def rows(core, first=0, count=HALF):
        return pl.ds(core * HALF + first, count)

    line = [(dx, core) for dx in range(X) for core in (c, other) if (dx, core) != (0, c)]
    sib = at(core=other)

    barrier = pltpu.get_barrier_semaphore()
    peers = [at(dz=d) for d in range(1, Z)] + [at(dy=d) for d in range(1, Y)]
    peers += [at(dx=dx, core=core) for dx, core in line]
    for to in peers:
        pl.semaphore_signal(barrier, inc=1, device_id=to, device_id_type=MESH)

    for i in range(X):
        @pl.when(x == i)
        def _():
            part = feat[:, CHIP * i:CHIP * (i + 1)].astype(jnp.float32)
            none = jnp.zeros_like(part)
            ft[...] = jnp.concatenate([part, none] if c == 0 else [none, part], 0).T.astype(jnp.bfloat16)
    pl.semaphore_wait(barrier, len(peers))

    send(ft.at[theirs], half_x.at[pl.ds(0, WIDTH[other])], h_sem.at[0], h_sem.at[1], sib)

    for q in range(4):
        for dx, k in ((1, q), (-1, 3 - q)):
            send(a_in.at[pl.ds(k * CHUNK, CHUNK)], a_all.at[x, rows(c, k * CHUNK, CHUNK)],
                 as_sem.at[0], a_sem.at[x, k], at(dx=dx))
    send(a_in, a_all.at[x, rows(c)], as_sem.at[2], c_sem.at[x], sib)
    own_a = pltpu.make_async_copy(a_in, a_all.at[x, rows(c)], l_sem.at[0])
    own_a.start()

    def gather_start(h, src):
        b = blk()
        for dy, dz in DIRECT:
            send(src, block(h, b), s_sem.at[h], r_sem.at[h, b], at(dy=dy, dz=dz))

    def gather_relay(h):
        for o in RELAYS:
            b = blk(-o[0], -o[1])
            ref = block(h, b)
            arrived(ref, r_sem.at[h, b])
            for k in KIDS[o]:
                send(ref, ref, s_sem.at[h], r_sem.at[h, b], at(dy=k[0] - o[0], dz=k[1] - o[1]))

    def gather_rest(h):
        for o in LEAVES:
            b = blk(-o[0], -o[1])
            arrived(block(h, b), r_sem.at[h, b])

    def tile_chunk(s, k):
        ref = a_all.at[s, rows(c, k * CHUNK, CHUNK)]
        arrived(ref, a_sem.at[s, k])
        return ref

    def compute(h):
        for k in range(SLOTS):
            on = (mbuf[2 * h, 1:2, :] > k).astype(jnp.float32).astype(jnp.bfloat16)
            lhs[0:w, k * TILE:(k + 1) * TILE] = xgs[h][sm[h, k, 0], 0:w] * on
        acc = lax.dot_general(lhs[0:w, :], a_all[h], (((1,), (1,)), ((), ())),
                              preferred_element_type=jnp.float32)
        degree = mbuf[2 * h, 0:1, :] + mbuf[2 * h + 1, 0:1, :]
        val = acc * lax.rsqrt(degree.astype(jnp.float32))
        if h < HOPS - 1:
            ybuf[h, 0:w] = val.astype(jnp.bfloat16)
            xgs[h + 1][blk(), 0:w] = val.astype(jnp.bfloat16)
            gather_start(h + 1, ybuf.at[h, pl.ds(0, w)])
        wide = jnp.concatenate([val, val], 0) if w == HALF else val
        tbuf[h] = wide.T.astype(jnp.bfloat16)

        @pl.when(x == h)
        def _():
            obuf[g] = tbuf[h, c * HALF:(c + 1) * HALF]
            send(tbuf.at[h, rows(other)], obuf.at[g], os_sem.at[0], o_sem.at[g], sib)

        @pl.when(x != h)
        def _():
            for core in (0, 1):
                send(tbuf.at[h, rows(core)], obuf.at[g], os_sem.at[0], o_sem.at[g], (h, (sh // 2) * 2 + core))

    arrived(half_x.at[pl.ds(0, w)], h_sem.at[1])
    xg0[blk(), 0:w] = (ft[FIRST[c]:FIRST[c] + w].astype(jnp.float32) + half_x[0:w].astype(jnp.float32)).astype(jnp.bfloat16)
    gather_start(0, block(0, blk()))
    lane = lax.broadcasted_iota(jnp.int32, (SLOTS, BLOCKS), 1)
    col = jnp.sum(jnp.where(lane == sh // 2, cols[0], 0), axis=1, keepdims=True)
    col = (col & (Y - 1)) * Z + (col >> 2)
    meta[pl.ds(COLS_AT, SLOTS), :] = jnp.broadcast_to(col, (SLOTS, TILE))
    count = jnp.sum(jnp.where(lane[0:1] == sh // 2, live[...], 0), axis=1, keepdims=True)
    d = deg[...]
    none = jnp.zeros_like(d)
    meta[0:1, :] = jnp.concatenate([d, none] if c == 0 else [none, d], 1)
    meta[1:2, :] = jnp.broadcast_to(count, (1, TILE))
    for dx, core in line:
        send(meta, mbuf.at[g], ms_sem.at[0], m_sem.at[g], at(dx=dx, core=core))
    mbuf[g] = meta[...]
    gather_relay(0)

    left, right, far_x = (x - 1) % X, (x + 1) % X, (x + 2) % X
    for q in range(2):
        for s, k, dx in ((left, q, 1), (right, 3 - q, -1)):
            ref = tile_chunk(s, k)
            send(ref, ref, as_sem.at[1], a_sem.at[s, k], at(dx=dx))
    for s, ks in ((left, (2, 3)), (right, (1, 0)), (far_x, (0, 1, 2, 3))):
        for k in ks:
            tile_chunk(s, k)
        piece = a_all.at[s, rows(c)]
        send(piece, piece, as_sem.at[2], c_sem.at[s], sib)
    for dx, core in line:
        p = 2 * ((x + dx) % X) + core
        arrived(mbuf.at[p], m_sem.at[p])
    to_sm = [pltpu.make_async_copy(mbuf.at[2 * s, pl.ds(COLS_AT, SLOTS)], sm.at[s], l_sem.at[1 + s]) for s in range(X)]
    for copy in to_sm:
        copy.start()
    own_a.wait()
    for copy in to_sm:
        copy.wait()
    for h in range(HOPS):
        if h:
            gather_relay(h)
        gather_rest(h)
        arrived(a_all.at[h, rows(other)], c_sem.at[h])
        compute(h)

    for dx, core in line:
        p = 2 * ((x + dx) % X) + core
        arrived(obuf.at[p], o_sem.at[p])
    low = lax.broadcasted_iota(jnp.int32, (HALF, TILE), 1) < HALF
    for i in range(0, X, 2):
        p0, p1, q0, q1 = (obuf[2 * i + j].astype(jnp.float32) for j in range(4))
        turned = jnp.concatenate([p1[:, HALF:], p1[:, :HALF]], 1)
        at0 = CHIP * i
        out[:, at0:at0 + TILE] = jnp.where(low, p0, turned).astype(jnp.bfloat16)
        out[:, at0 + TILE:at0 + 2 * TILE] = jnp.where(low, turned, q0).astype(jnp.bfloat16)
        out[:, at0 + 2 * TILE:at0 + 3 * TILE] = q1.astype(jnp.bfloat16)

    arrived(half_x.at[pl.ds(0, WIDTH[other])], h_sem.at[0])
    arrived(a_all.at[0], as_sem.at[0])
    arrived(a_all.at[0, pl.ds(0, HALF)], as_sem.at[1])
    arrived(a_all.at[pl.ds(0, 2)], as_sem.at[2])
    arrived(mbuf.at[pl.ds(0, 7)], ms_sem.at[0])
    arrived(obuf.at[pl.ds(0, 7)], os_sem.at[0])
    for h in range(HOPS):
        arrived(xgs[h].at[pl.ds(0, 31), pl.ds(0, w)], s_sem.at[h])


def per_device(features, tile_cols, live_tiles, tile_values, degrees):
    a_in = tile_values[0].reshape(HALF, SLOTS * TILE)
    cols = jnp.swapaxes(tile_cols, 1, 2)
    vm = pl.BlockSpec(memory_space=pltpu.VMEM)
    dma = pltpu.SemaphoreType.DMA
    slab = pltpu.VMEM((BLOCKS, TILE, TILE), jnp.bfloat16)
    res = pl.pallas_call(
        kernel,
        out_shape=jax.ShapeDtypeStruct((HALF, X * CHIP), jnp.bfloat16),
        in_specs=[vm] * 5,
        out_specs=vm,
        scratch_shapes=[
            slab, slab, slab, slab,
            pltpu.VMEM((X, TILE, SLOTS * TILE), jnp.bfloat16),
            pltpu.VMEM((TILE, SLOTS * TILE), jnp.bfloat16),
            pltpu.VMEM((HOPS, TILE, TILE), jnp.bfloat16),
            pltpu.VMEM((HOPS, TILE, TILE), jnp.bfloat16),
            pltpu.VMEM((TILE, TILE), jnp.bfloat16),
            pltpu.VMEM((CHIP, TILE), jnp.bfloat16),
            pltpu.VMEM((24, TILE), jnp.int32),
            pltpu.VMEM((8, 24, TILE), jnp.int32),
            pltpu.VMEM((8, HALF, TILE), jnp.bfloat16),
            pltpu.SMEM((X, SLOTS, TILE), jnp.int32),
            dma((HOPS, BLOCKS)), dma((HOPS,)), dma((X, 4)), dma((X,)), dma((3,)),
            dma((8,)), dma((1,)), dma((8,)), dma((1,)), dma((2,)), dma((5,)),
        ],
        compiler_params=pltpu.CompilerParams(collective_id=0, has_side_effects=True,
                                             vmem_limit_bytes=40 * 1024 * 1024),
        name="propagate",
    )(features, cols, live_tiles, degrees, a_in)
    return res[None]


def solution(mesh):
    in_specs = (
        P("shard", None),
        P("section", None, None),
        P("section", None),
        P("section", "shard", None, None),
        P("section", "shard"),
    )
    return jax.shard_map(per_device, mesh=mesh, in_specs=in_specs,
                         out_specs=P("section", "shard", None), check_vma=False)
```

```python
import jax
import jax.numpy as jnp
from jax import lax
from jax.experimental import pallas as pl
from jax.experimental.pallas import tpu as pltpu
from jax.sharding import PartitionSpec as P

MESH = pl.DeviceIdType.MESH
X, Y, Z = 4, 4, 8
HOPS = 4
TILE = 128
SLOTS = 16
BLOCKS = Y * Z
HALF = 64
CHUNK = 16
CHIP = 192
WIDTH = (64, 128)
FIRST = (0, 64)
COLS_AT = 8
DYS = (0, 1, -1, 2)
DZS = (0, 1, -1, 2, -2, 3, -3, 4)


def parent(dy, dz):
    if dy == 0 or dz == 0:
        return (0, 0)
    if abs(dz) == 1 or (abs(dz) == 2 and dy == 2):
        return (dy, 0)
    return (0, dz)


def far(o):
    return abs(o[0]) + abs(o[1])


OFFSETS = [(dy, dz) for dz in DZS for dy in DYS if dy or dz]
KIDS = {}
for _o in sorted(OFFSETS, key=lambda o: -far(o)):
    KIDS.setdefault(parent(*_o), []).append(_o)
DIRECT = sorted(KIDS.pop((0, 0)), key=lambda o: (o not in KIDS, -far(o)))
RELAYS = sorted(KIDS, key=far)
LEAVES = [o for o in sorted(OFFSETS, key=lambda o: (far(o) + far(parent(*o)), far(o))) if o not in KIDS]


def send(src, dst, ssem, rsem, to):
    pltpu.make_async_remote_copy(src_ref=src, dst_ref=dst, send_sem=ssem, recv_sem=rsem,
                                 device_id=to, device_id_type=MESH).start()


def arrived(ref, sem):
    pltpu.make_async_copy(ref, ref, sem).wait()


def kernel(*refs):
    core = lax.axis_index("shard") % 2
    for c in (0, 1):
        @pl.when(core == c)
        def _():
            run(c, *refs)


def run(c, feat, cols, live, deg, a_in, out, xg0, xg1, xg2, xg3, a_all, lhs, ybuf, tbuf, half_x, ft, meta, mbuf, obuf, sm,
        r_sem, s_sem, a_sem, c_sem, as_sem, m_sem, ms_sem, o_sem, os_sem, h_sem, l_sem):
    x = lax.axis_index("section")
    sh = lax.axis_index("shard")
    z, y = sh // 8, (sh // 2) % 4
    g = 2 * x + c
    xgs = (xg0, xg1, xg2, xg3)
    other = 1 - c
    w = WIDTH[c]
    mine, theirs = pl.ds(FIRST[c], w), pl.ds(FIRST[other], WIDTH[other])

    def at(dx=0, dy=0, dz=0, core=c):
        return ((x + dx) % X, ((z + dz) % Z) * 8 + ((y + dy) % Y) * 2 + core)

    def blk(dy=0, dz=0):
        return ((y + dy) % Y) * Z + (z + dz) % Z

    def block(h, b):
        return xgs[h].at[b, pl.ds(0, w)]

    def rows(core, first=0, count=HALF):
        return pl.ds(core * HALF + first, count)

    line = [(dx, core) for dx in range(X) for core in (c, other) if (dx, core) != (0, c)]
    sib = at(core=other)

    barrier = pltpu.get_barrier_semaphore()
    peers = [at(dz=d) for d in range(1, Z)] + [at(dy=d) for d in range(1, Y)]
    peers += [at(dx=dx, core=core) for dx, core in line]
    for to in peers:
        pl.semaphore_signal(barrier, inc=1, device_id=to, device_id_type=MESH)

    for i in range(X):
        @pl.when(x == i)
        def _():
            part = feat[:, CHIP * i:CHIP * (i + 1)].astype(jnp.float32)
            none = jnp.zeros_like(part)
            ft[...] = jnp.concatenate([part, none] if c == 0 else [none, part], 0).T.astype(jnp.bfloat16)
    pl.semaphore_wait(barrier, len(peers))

    send(ft.at[theirs], half_x.at[pl.ds(0, WIDTH[other])], h_sem.at[0], h_sem.at[1], sib)

    for q in range(4):
        for dx, k in ((1, q), (-1, 3 - q)):
            send(a_in.at[pl.ds(k * CHUNK, CHUNK)], a_all.at[x, rows(c, k * CHUNK, CHUNK)],
                 as_sem.at[0], a_sem.at[x, k], at(dx=dx))
    send(a_in, a_all.at[x, rows(c)], as_sem.at[2], c_sem.at[x], sib)
    own_a = pltpu.make_async_copy(a_in, a_all.at[x, rows(c)], l_sem.at[0])
    own_a.start()

    def gather_start(h, src):
        b = blk()
        for dy, dz in DIRECT:
            send(src, block(h, b), s_sem.at[h], r_sem.at[h, b], at(dy=dy, dz=dz))

    def gather_relay(h):
        for o in RELAYS:
            b = blk(-o[0], -o[1])
            ref = block(h, b)
            arrived(ref, r_sem.at[h, b])
            for k in KIDS[o]:
                send(ref, ref, s_sem.at[h], r_sem.at[h, b], at(dy=k[0] - o[0], dz=k[1] - o[1]))

    def gather_rest(h):
        for o in LEAVES:
            b = blk(-o[0], -o[1])
            arrived(block(h, b), r_sem.at[h, b])

    def tile_chunk(s, k):
        ref = a_all.at[s, rows(c, k * CHUNK, CHUNK)]
        arrived(ref, a_sem.at[s, k])
        return ref

    def compute(h):
        for k in range(SLOTS):
            on = (mbuf[2 * h, 1:2, :] > k).astype(jnp.float32).astype(jnp.bfloat16)
            lhs[0:w, k * TILE:(k + 1) * TILE] = xgs[h][sm[h, k, 0], 0:w] * on
        acc = lax.dot_general(lhs[0:w, :], a_all[h], (((1,), (1,)), ((), ())),
                              preferred_element_type=jnp.float32)
        degree = mbuf[2 * h, 0:1, :] + mbuf[2 * h + 1, 0:1, :]
        val = acc * lax.rsqrt(degree.astype(jnp.float32))
        if h < HOPS - 1:
            ybuf[h, 0:w] = val.astype(jnp.bfloat16)
            xgs[h + 1][blk(), 0:w] = val.astype(jnp.bfloat16)
            gather_start(h + 1, ybuf.at[h, pl.ds(0, w)])
        wide = jnp.concatenate([val, val], 0) if w == HALF else val
        tbuf[h] = wide.T.astype(jnp.bfloat16)

        @pl.when(x == h)
        def _():
            obuf[g] = tbuf[h, c * HALF:(c + 1) * HALF]
            send(tbuf.at[h, rows(other)], obuf.at[g], os_sem.at[0], o_sem.at[g], sib)

        @pl.when(x != h)
        def _():
            for core in (0, 1):
                send(tbuf.at[h, rows(core)], obuf.at[g], os_sem.at[0], o_sem.at[g], (h, (sh // 2) * 2 + core))

    arrived(half_x.at[pl.ds(0, w)], h_sem.at[1])
    xg0[blk(), 0:w] = (ft[FIRST[c]:FIRST[c] + w].astype(jnp.float32) + half_x[0:w].astype(jnp.float32)).astype(jnp.bfloat16)
    gather_start(0, block(0, blk()))
    lane = lax.broadcasted_iota(jnp.int32, (SLOTS, BLOCKS), 1)
    col = jnp.sum(jnp.where(lane == sh // 2, cols[0], 0), axis=1, keepdims=True)
    col = (col & (Y - 1)) * Z + (col >> 2)
    meta[pl.ds(COLS_AT, SLOTS), :] = jnp.broadcast_to(col, (SLOTS, TILE))
    count = jnp.sum(jnp.where(lane[0:1] == sh // 2, live[...], 0), axis=1, keepdims=True)
    d = deg[...]
    none = jnp.zeros_like(d)
    meta[0:1, :] = jnp.concatenate([d, none] if c == 0 else [none, d], 1)
    meta[1:2, :] = jnp.broadcast_to(count, (1, TILE))
    for dx, core in line:
        send(meta, mbuf.at[g], ms_sem.at[0], m_sem.at[g], at(dx=dx, core=core))
    mbuf[g] = meta[...]
    gather_relay(0)

    left, right, far_x = (x - 1) % X, (x + 1) % X, (x + 2) % X
    for q in range(2):
        for s, k, dx in ((left, q, 1), (right, 3 - q, -1)):
            ref = tile_chunk(s, k)
            send(ref, ref, as_sem.at[1], a_sem.at[s, k], at(dx=dx))
    for s, ks in ((left, (2, 3)), (right, (1, 0)), (far_x, (0, 1, 2, 3))):
        for k in ks:
            tile_chunk(s, k)
        piece = a_all.at[s, rows(c)]
        send(piece, piece, as_sem.at[2], c_sem.at[s], sib)
    for dx, core in line:
        p = 2 * ((x + dx) % X) + core
        arrived(mbuf.at[p], m_sem.at[p])
    to_sm = [pltpu.make_async_copy(mbuf.at[2 * s, pl.ds(COLS_AT, SLOTS)], sm.at[s], l_sem.at[1 + s]) for s in range(X)]
    for copy in to_sm:
        copy.start()
    own_a.wait()
    for copy in to_sm:
        copy.wait()
    for h in range(HOPS):
        if h:
            gather_relay(h)
        gather_rest(h)
        arrived(a_all.at[h, rows(other)], c_sem.at[h])
        compute(h)

    for dx, core in line:
        p = 2 * ((x + dx) % X) + core
        arrived(obuf.at[p], o_sem.at[p])
    low = lax.broadcasted_iota(jnp.int32, (HALF, TILE), 1) < HALF
    for i in range(0, X, 2):
        p0, p1, q0, q1 = (obuf[2 * i + j].astype(jnp.float32) for j in range(4))
        turned = jnp.concatenate([p1[:, HALF:], p1[:, :HALF]], 1)
        at0 = CHIP * i
        out[:, at0:at0 + TILE] = jnp.where(low, p0, turned).astype(jnp.bfloat16)
        out[:, at0 + TILE:at0 + 2 * TILE] = jnp.where(low, turned, q0).astype(jnp.bfloat16)
        out[:, at0 + 2 * TILE:at0 + 3 * TILE] = q1.astype(jnp.bfloat16)

    arrived(half_x.at[pl.ds(0, WIDTH[other])], h_sem.at[0])
    arrived(a_all.at[0], as_sem.at[0])
    arrived(a_all.at[0, pl.ds(0, HALF)], as_sem.at[1])
    arrived(a_all.at[pl.ds(0, 2)], as_sem.at[2])
    arrived(mbuf.at[pl.ds(0, 7)], ms_sem.at[0])
    arrived(obuf.at[pl.ds(0, 7)], os_sem.at[0])
    for h in range(HOPS):
        arrived(xgs[h].at[pl.ds(0, 31), pl.ds(0, w)], s_sem.at[h])


def per_device(features, tile_cols, live_tiles, tile_values, degrees):
    a_in = tile_values[0].reshape(HALF, SLOTS * TILE)
    cols = jnp.swapaxes(tile_cols, 1, 2)
    vm = pl.BlockSpec(memory_space=pltpu.VMEM)
    dma = pltpu.SemaphoreType.DMA
    slab = pltpu.VMEM((BLOCKS, TILE, TILE), jnp.bfloat16)
    res = pl.pallas_call(
        kernel,
        out_shape=jax.ShapeDtypeStruct((HALF, X * CHIP), jnp.bfloat16),
        in_specs=[vm] * 5,
        out_specs=vm,
        scratch_shapes=[
            slab, slab, slab, slab,
            pltpu.VMEM((X, TILE, SLOTS * TILE), jnp.bfloat16),
            pltpu.VMEM((TILE, SLOTS * TILE), jnp.bfloat16),
            pltpu.VMEM((HOPS, TILE, TILE), jnp.bfloat16),
            pltpu.VMEM((HOPS, TILE, TILE), jnp.bfloat16),
            pltpu.VMEM((TILE, TILE), jnp.bfloat16),
            pltpu.VMEM((CHIP, TILE), jnp.bfloat16),
            pltpu.VMEM((24, TILE), jnp.int32),
            pltpu.VMEM((8, 24, TILE), jnp.int32),
            pltpu.VMEM((8, HALF, TILE), jnp.bfloat16),
            pltpu.SMEM((X, SLOTS, TILE), jnp.int32),
            dma((HOPS, BLOCKS)), dma((HOPS,)), dma((X, 4)), dma((X,)), dma((3,)),
            dma((8,)), dma((1,)), dma((8,)), dma((1,)), dma((2,)), dma((5,)),
        ],
        compiler_params=pltpu.CompilerParams(collective_id=0, has_side_effects=True,
                                             vmem_limit_bytes=40 * 1024 * 1024),
        name="propagate",
    )(features, cols, live_tiles, degrees, a_in)
    return res[None]


def solution(mesh):
    in_specs = (
        P("shard", None),
        P("section", None, None),
        P("section", None),
        P("section", "shard", None, None),
        P("section", "shard"),
    )
    return jax.shard_map(per_device, mesh=mesh, in_specs=in_specs,
                         out_specs=P("section", "shard", None), check_vma=False)
```

```python
import jax
import jax.numpy as jnp
from jax import lax
from jax.experimental import pallas as pl
from jax.experimental.pallas import tpu as pltpu
from jax.sharding import PartitionSpec as P

MESH = pl.DeviceIdType.MESH
X, Y, Z = 4, 4, 8
HOPS = 4
TILE = 128
SLOTS = 16
BLOCKS = Y * Z
HALF = 64
CHUNK = 16
CHIP = 192
WIDTH = (64, 128)
FIRST = (0, 64)
COLS_AT = 8
DYS = (0, 1, -1, 2)
DZS = (0, 1, -1, 2, -2, 3, -3, 4)


def parent(dy, dz):
    if dy == 0 or dz == 0:
        return (0, 0)
    if abs(dz) <= 2:
        return (dy, 0)
    return (0, dz)


def far(o):
    return abs(o[0]) + abs(o[1])


OFFSETS = [(dy, dz) for dz in DZS for dy in DYS if dy or dz]
KIDS = {}
for _o in sorted(OFFSETS, key=lambda o: -far(o)):
    KIDS.setdefault(parent(*_o), []).append(_o)
DIRECT = sorted(KIDS.pop((0, 0)), key=lambda o: (o not in KIDS, -far(o)))
RELAYS = sorted(KIDS, key=far)
LEAVES = [o for o in sorted(OFFSETS, key=lambda o: (far(o) + far(parent(*o)), far(o))) if o not in KIDS]


def send(src, dst, ssem, rsem, to):
    pltpu.make_async_remote_copy(src_ref=src, dst_ref=dst, send_sem=ssem, recv_sem=rsem,
                                 device_id=to, device_id_type=MESH).start()


def arrived(ref, sem):
    pltpu.make_async_copy(ref, ref, sem).wait()


def kernel(*refs):
    core = lax.axis_index("shard") % 2
    for c in (0, 1):
        @pl.when(core == c)
        def _():
            run(c, *refs)


def run(c, feat, cols, live, deg, a_in, out, xg0, xg1, xg2, xg3, a_all, ybuf, tbuf, half_x, ft, meta, mbuf, obuf, a_t, sm,
        r_sem, s_sem, a_sem, c_sem, as_sem, m_sem, ms_sem, o_sem, os_sem, h_sem, l_sem):
    x = lax.axis_index("section")
    sh = lax.axis_index("shard")
    z, y = sh // 8, (sh // 2) % 4
    g = 2 * x + c
    xgs = (xg0, xg1, xg2, xg3)
    other = 1 - c
    w = WIDTH[c]
    mine, theirs = pl.ds(FIRST[c], w), pl.ds(FIRST[other], WIDTH[other])

    def at(dx=0, dy=0, dz=0, core=c):
        return ((x + dx) % X, ((z + dz) % Z) * 8 + ((y + dy) % Y) * 2 + core)

    def blk(dy=0, dz=0):
        return ((y + dy) % Y) * Z + (z + dz) % Z

    def block(h, b):
        return xgs[h].at[b, pl.ds(0, w)]

    def rows(core, first=0, count=HALF):
        return pl.ds(core * HALF + first, count)

    line = [(dx, core) for dx in range(X) for core in (c, other) if (dx, core) != (0, c)]
    sib = at(core=other)

    barrier = pltpu.get_barrier_semaphore()
    peers = [at(dz=d) for d in range(1, Z)] + [at(dy=d) for d in range(1, Y)]
    peers += [at(dx=dx, core=core) for dx, core in line]
    for to in peers:
        pl.semaphore_signal(barrier, inc=1, device_id=to, device_id_type=MESH)

    for i in range(X):
        @pl.when(x == i)
        def _():
            part = feat[:, CHIP * i:CHIP * (i + 1)].astype(jnp.float32)
            none = jnp.zeros_like(part)
            ft[...] = jnp.concatenate([part, none] if c == 0 else [none, part], 0).T.astype(jnp.bfloat16)
    pl.semaphore_wait(barrier, len(peers))

    send(ft.at[theirs], half_x.at[pl.ds(0, WIDTH[other])], h_sem.at[0], h_sem.at[1], sib)

    for q in range(4):
        for dx, k in ((1, q), (-1, 3 - q)):
            send(a_in.at[pl.ds(k * CHUNK, CHUNK)], a_all.at[x, rows(c, k * CHUNK, CHUNK)],
                 as_sem.at[0], a_sem.at[x, k], at(dx=dx))
    send(a_in, a_all.at[x, rows(c)], as_sem.at[2], c_sem.at[x], sib)
    own_a = pltpu.make_async_copy(a_in, a_all.at[x, rows(c)], l_sem.at[0])
    own_a.start()

    def gather_start(h, src):
        b = blk()
        for dy, dz in DIRECT:
            send(src, block(h, b), s_sem.at[h], r_sem.at[h, b], at(dy=dy, dz=dz))

    def gather_relay(h, relays=RELAYS):
        for o in relays:
            b = blk(-o[0], -o[1])
            ref = block(h, b)
            arrived(ref, r_sem.at[h, b])
            for k in KIDS[o]:
                send(ref, ref, s_sem.at[h], r_sem.at[h, b], at(dy=k[0] - o[0], dz=k[1] - o[1]))

    def gather_rest(h):
        for o in LEAVES:
            b = blk(-o[0], -o[1])
            arrived(block(h, b), r_sem.at[h, b])

    def tile_chunk(s, k):
        ref = a_all.at[s, rows(c, k * CHUNK, CHUNK)]
        arrived(ref, a_sem.at[s, k])
        return ref

    def prepare(h):
        a_t[...] = a_all[h].T
        for k in range(SLOTS):
            on = (mbuf[2 * h, 1:2, :] > k).astype(jnp.float32).astype(jnp.bfloat16)
            a_t[k * TILE:(k + 1) * TILE, :] = a_t[k * TILE:(k + 1) * TILE, :] * on
        degree = mbuf[2 * h, 0:1, :] + mbuf[2 * h + 1, 0:1, :]
        return lax.rsqrt(degree.astype(jnp.float32))

    def compute(h, scale):
        acc = jnp.zeros((w, TILE), jnp.float32)
        for k in range(0, SLOTS, 4):
            src = jnp.concatenate([xgs[h][sm[h, k + i, 0], 0:w] for i in range(4)], axis=1)
            acc = acc + jnp.dot(src, a_t[k * TILE:(k + 4) * TILE, :], preferred_element_type=jnp.float32)
        val = acc * scale
        if h < HOPS - 1:
            ybuf[h, 0:w] = val.astype(jnp.bfloat16)
            xgs[h + 1][blk(), 0:w] = val.astype(jnp.bfloat16)
            gather_start(h + 1, ybuf.at[h, pl.ds(0, w)])
        wide = jnp.concatenate([val, val], 0) if w == HALF else val
        tbuf[h] = wide.T.astype(jnp.bfloat16)

        @pl.when(x == h)
        def _():
            obuf[g] = tbuf[h, c * HALF:(c + 1) * HALF]
            send(tbuf.at[h, rows(other)], obuf.at[g], os_sem.at[0], o_sem.at[g], sib)

        @pl.when(x != h)
        def _():
            for core in (0, 1):
                send(tbuf.at[h, rows(core)], obuf.at[g], os_sem.at[0], o_sem.at[g], (h, (sh // 2) * 2 + core))

    arrived(half_x.at[pl.ds(0, w)], h_sem.at[1])
    xg0[blk(), 0:w] = (ft[FIRST[c]:FIRST[c] + w].astype(jnp.float32) + half_x[0:w].astype(jnp.float32)).astype(jnp.bfloat16)
    gather_start(0, block(0, blk()))
    lane = lax.broadcasted_iota(jnp.int32, (SLOTS, BLOCKS), 1)
    col = jnp.sum(jnp.where(lane == sh // 2, cols[0], 0), axis=1, keepdims=True)
    col = (col & (Y - 1)) * Z + (col >> 2)
    meta[pl.ds(COLS_AT, SLOTS), :] = jnp.broadcast_to(col, (SLOTS, TILE))
    count = jnp.sum(jnp.where(lane[0:1] == sh // 2, live[...], 0), axis=1, keepdims=True)
    d = deg[...]
    none = jnp.zeros_like(d)
    meta[0:1, :] = jnp.concatenate([d, none] if c == 0 else [none, d], 1)
    meta[1:2, :] = jnp.broadcast_to(count, (1, TILE))
    for dx, core in line:
        send(meta, mbuf.at[g], ms_sem.at[0], m_sem.at[g], at(dx=dx, core=core))
    mbuf[g] = meta[...]
    gather_relay(0, RELAYS[:3])

    left, right, far_x = (x - 1) % X, (x + 1) % X, (x + 2) % X
    for q in range(2):
        for s, k, dx in ((left, q, 1), (right, 3 - q, -1)):
            ref = tile_chunk(s, k)
            send(ref, ref, as_sem.at[1], a_sem.at[s, k], at(dx=dx))
    gather_relay(0, RELAYS[3:])

    for s, ks in ((left, (2, 3)), (right, (1, 0)), (far_x, (0, 1, 2, 3))):
        for k in ks:
            tile_chunk(s, k)
        piece = a_all.at[s, rows(c)]
        send(piece, piece, as_sem.at[2], c_sem.at[s], sib)
    for dx, core in line:
        p = 2 * ((x + dx) % X) + core
        arrived(mbuf.at[p], m_sem.at[p])
    to_sm = [pltpu.make_async_copy(mbuf.at[2 * s, pl.ds(COLS_AT, SLOTS)], sm.at[s], l_sem.at[1 + s]) for s in range(X)]
    for copy in to_sm:
        copy.start()
    own_a.wait()
    for copy in to_sm:
        copy.wait()
    for h in range(HOPS):
        if h:
            gather_relay(h)
        arrived(a_all.at[h, rows(other)], c_sem.at[h])
        scale = prepare(h)
        gather_rest(h)
        compute(h, scale)

    for dx, core in line:
        p = 2 * ((x + dx) % X) + core
        arrived(obuf.at[p], o_sem.at[p])
    low = lax.broadcasted_iota(jnp.int32, (HALF, TILE), 1) < HALF
    for i in range(0, X, 2):
        p0, p1, q0, q1 = (obuf[2 * i + j].astype(jnp.float32) for j in range(4))
        turned = jnp.concatenate([p1[:, HALF:], p1[:, :HALF]], 1)
        at0 = CHIP * i
        out[:, at0:at0 + TILE] = jnp.where(low, p0, turned).astype(jnp.bfloat16)
        out[:, at0 + TILE:at0 + 2 * TILE] = jnp.where(low, turned, q0).astype(jnp.bfloat16)
        out[:, at0 + 2 * TILE:at0 + 3 * TILE] = q1.astype(jnp.bfloat16)

    arrived(half_x.at[pl.ds(0, WIDTH[other])], h_sem.at[0])
    arrived(a_all.at[0], as_sem.at[0])
    arrived(a_all.at[0, pl.ds(0, HALF)], as_sem.at[1])
    arrived(a_all.at[pl.ds(0, 2)], as_sem.at[2])
    arrived(mbuf.at[pl.ds(0, 7)], ms_sem.at[0])
    arrived(obuf.at[pl.ds(0, 7)], os_sem.at[0])
    for h in range(HOPS):
        arrived(xgs[h].at[pl.ds(0, 31), pl.ds(0, w)], s_sem.at[h])


def per_device(features, tile_cols, live_tiles, tile_values, degrees):
    a_in = tile_values[0].reshape(HALF, SLOTS * TILE)
    cols = jnp.swapaxes(tile_cols, 1, 2)
    vm = pl.BlockSpec(memory_space=pltpu.VMEM)
    dma = pltpu.SemaphoreType.DMA
    slab = pltpu.VMEM((BLOCKS, TILE, TILE), jnp.bfloat16)
    res = pl.pallas_call(
        kernel,
        out_shape=jax.ShapeDtypeStruct((HALF, X * CHIP), jnp.bfloat16),
        in_specs=[vm] * 5,
        out_specs=vm,
        scratch_shapes=[
            slab, slab, slab, slab,
            pltpu.VMEM((X, TILE, SLOTS * TILE), jnp.bfloat16),
            pltpu.VMEM((HOPS, TILE, TILE), jnp.bfloat16),
            pltpu.VMEM((HOPS, TILE, TILE), jnp.bfloat16),
            pltpu.VMEM((TILE, TILE), jnp.bfloat16),
            pltpu.VMEM((CHIP, TILE), jnp.bfloat16),
            pltpu.VMEM((24, TILE), jnp.int32),
            pltpu.VMEM((8, 24, TILE), jnp.int32),
            pltpu.VMEM((8, HALF, TILE), jnp.bfloat16),
            pltpu.VMEM((SLOTS * TILE, TILE), jnp.bfloat16),
            pltpu.SMEM((X, SLOTS, TILE), jnp.int32),
            dma((HOPS, BLOCKS)), dma((HOPS,)), dma((X, 4)), dma((X,)), dma((3,)),
            dma((8,)), dma((1,)), dma((8,)), dma((1,)), dma((2,)), dma((5,)),
        ],
        compiler_params=pltpu.CompilerParams(collective_id=0, has_side_effects=True,
                                             vmem_limit_bytes=40 * 1024 * 1024),
        name="propagate",
    )(features, cols, live_tiles, degrees, a_in)
    return res[None]


def solution(mesh):
    in_specs = (
        P("shard", None),
        P("section", None, None),
        P("section", None),
        P("section", "shard", None, None),
        P("section", "shard"),
    )
    return jax.shard_map(per_device, mesh=mesh, in_specs=in_specs,
                         out_specs=P("section", "shard", None), check_vma=False)
```

```python
import jax
import jax.numpy as jnp
from jax import lax
from jax.experimental import pallas as pl
from jax.experimental.pallas import tpu as pltpu
from jax.sharding import PartitionSpec as P

MESH = pl.DeviceIdType.MESH
X, Y, Z = 4, 4, 8
HOPS = 4
TILE = 128
SLOTS = 16
BLOCKS = Y * Z
HALF = 64
CHUNK = 16
CHIP = 192
WIDTH = (64, 128)
FIRST = (0, 64)
COLS_AT = 8
DYS = (0, 1, -1, 2)
DZS = (0, 1, -1, 2, -2, 3, -3, 4)


def parent(dy, dz):
    if dy == 0 or dz == 0:
        return (0, 0)
    if abs(dz) <= 2:
        return (dy, 0)
    return (0, dz)


def far(o):
    return abs(o[0]) + abs(o[1])


OFFSETS = [(dy, dz) for dz in DZS for dy in DYS if dy or dz]
KIDS = {}
for _o in sorted(OFFSETS, key=lambda o: -far(o)):
    KIDS.setdefault(parent(*_o), []).append(_o)
DIRECT = sorted(KIDS.pop((0, 0)), key=lambda o: (o not in KIDS, -far(o)))
RELAYS = sorted(KIDS, key=far)
LEAVES = [o for o in sorted(OFFSETS, key=lambda o: (far(o) + far(parent(*o)), far(o))) if o not in KIDS]


def send(src, dst, ssem, rsem, to):
    pltpu.make_async_remote_copy(src_ref=src, dst_ref=dst, send_sem=ssem, recv_sem=rsem,
                                 device_id=to, device_id_type=MESH).start()


def arrived(ref, sem):
    pltpu.make_async_copy(ref, ref, sem).wait()


def kernel(*refs):
    core = lax.axis_index("shard") % 2
    for c in (0, 1):
        @pl.when(core == c)
        def _():
            run(c, *refs)


def run(c, feat, cols, live, deg, a_in, out, xg0, xg1, xg2, xg3, a_all, ybuf, tbuf, half_x, ft, meta, mbuf, obuf, a_t, sm,
        r_sem, s_sem, a_sem, c_sem, as_sem, m_sem, ms_sem, o_sem, os_sem, h_sem, l_sem):
    x = lax.axis_index("section")
    sh = lax.axis_index("shard")
    z, y = sh // 8, (sh // 2) % 4
    g = 2 * x + c
    xgs = (xg0, xg1, xg2, xg3)
    other = 1 - c
    w = WIDTH[c]
    mine, theirs = pl.ds(FIRST[c], w), pl.ds(FIRST[other], WIDTH[other])

    def at(dx=0, dy=0, dz=0, core=c):
        return ((x + dx) % X, ((z + dz) % Z) * 8 + ((y + dy) % Y) * 2 + core)

    def blk(dy=0, dz=0):
        return ((y + dy) % Y) * Z + (z + dz) % Z

    def block(h, b):
        return xgs[h].at[b, pl.ds(0, w)]

    def rows(core, first=0, count=HALF):
        return pl.ds(core * HALF + first, count)

    line = [(dx, core) for dx in range(X) for core in (c, other) if (dx, core) != (0, c)]
    sib = at(core=other)

    barrier = pltpu.get_barrier_semaphore()
    peers = [at(dz=d) for d in (4, 3, 5, 2, 6, 1, 7)] + [at(dy=d) for d in (2, 1, 3)]
    peers += [at(dx=dx, core=core) for dx, core in line]
    for to in peers:
        pl.semaphore_signal(barrier, inc=1, device_id=to, device_id_type=MESH)

    for i in range(X):
        @pl.when(x == i)
        def _():
            part = feat[:, CHIP * i:CHIP * (i + 1)].astype(jnp.float32)
            none = jnp.zeros_like(part)
            ft[...] = jnp.concatenate([part, none] if c == 0 else [none, part], 0).T.astype(jnp.bfloat16)
    pl.semaphore_wait(barrier, len(peers))

    send(ft.at[theirs], half_x.at[pl.ds(0, WIDTH[other])], h_sem.at[0], h_sem.at[1], sib)

    for q in range(4):
        for dx, k in ((1, q), (-1, 3 - q)):
            send(a_in.at[pl.ds(k * CHUNK, CHUNK)], a_all.at[x, rows(c, k * CHUNK, CHUNK)],
                 as_sem.at[0], a_sem.at[x, k], at(dx=dx))
    send(a_in, a_all.at[x, rows(c)], as_sem.at[2], c_sem.at[x], sib)
    own_a = pltpu.make_async_copy(a_in, a_all.at[x, rows(c)], l_sem.at[0])
    own_a.start()

    def gather_start(h, src):
        b = blk()
        for dy, dz in DIRECT:
            send(src, block(h, b), s_sem.at[h], r_sem.at[h, b], at(dy=dy, dz=dz))

    def gather_relay(h, relays=RELAYS):
        for o in relays:
            b = blk(-o[0], -o[1])
            ref = block(h, b)
            arrived(ref, r_sem.at[h, b])
            for k in KIDS[o]:
                send(ref, ref, s_sem.at[h], r_sem.at[h, b], at(dy=k[0] - o[0], dz=k[1] - o[1]))

    def gather_rest(h):
        for o in LEAVES:
            b = blk(-o[0], -o[1])
            arrived(block(h, b), r_sem.at[h, b])

    def tile_chunk(s, k):
        ref = a_all.at[s, rows(c, k * CHUNK, CHUNK)]
        arrived(ref, a_sem.at[s, k])
        return ref

    def prepare(h):
        a_t[...] = a_all[h].T
        for k in range(SLOTS):
            on = (mbuf[2 * h, 1:2, :] > k).astype(jnp.float32).astype(jnp.bfloat16)
            a_t[k * TILE:(k + 1) * TILE, :] = a_t[k * TILE:(k + 1) * TILE, :] * on
        degree = mbuf[2 * h, 0:1, :] + mbuf[2 * h + 1, 0:1, :]
        return lax.rsqrt(degree.astype(jnp.float32))

    def compute(h, scale):
        acc = jnp.zeros((w, TILE), jnp.float32)
        for k in range(0, SLOTS, 4):
            src = jnp.concatenate([xgs[h][sm[h, k + i, 0], 0:w] for i in range(4)], axis=1)
            acc = acc + jnp.dot(src, a_t[k * TILE:(k + 4) * TILE, :], preferred_element_type=jnp.float32)
        val = acc * scale
        if h < HOPS - 1:
            ybuf[h, 0:w] = val.astype(jnp.bfloat16)
            xgs[h + 1][blk(), 0:w] = val.astype(jnp.bfloat16)
            gather_start(h + 1, ybuf.at[h, pl.ds(0, w)])
        wide = jnp.concatenate([val, val], 0) if w == HALF else val
        tbuf[h] = wide.T.astype(jnp.bfloat16)

        @pl.when(x == h)
        def _():
            obuf[g] = tbuf[h, c * HALF:(c + 1) * HALF]
            send(tbuf.at[h, rows(other)], obuf.at[g], os_sem.at[0], o_sem.at[g], sib)

        @pl.when(x != h)
        def _():
            for core in (1, 0):
                send(tbuf.at[h, rows(core)], obuf.at[g], os_sem.at[0], o_sem.at[g], (h, (sh // 2) * 2 + core))

    arrived(half_x.at[pl.ds(0, w)], h_sem.at[1])
    xg0[blk(), 0:w] = (ft[FIRST[c]:FIRST[c] + w].astype(jnp.float32) + half_x[0:w].astype(jnp.float32)).astype(jnp.bfloat16)
    gather_start(0, block(0, blk()))
    lane = lax.broadcasted_iota(jnp.int32, (SLOTS, BLOCKS), 1)
    col = jnp.sum(jnp.where(lane == sh // 2, cols[0], 0), axis=1, keepdims=True)
    col = (col & (Y - 1)) * Z + (col >> 2)
    meta[pl.ds(COLS_AT, SLOTS), :] = jnp.broadcast_to(col, (SLOTS, TILE))
    count = jnp.sum(jnp.where(lane[0:1] == sh // 2, live[...], 0), axis=1, keepdims=True)
    d = deg[...]
    none = jnp.zeros_like(d)
    meta[0:1, :] = jnp.concatenate([d, none] if c == 0 else [none, d], 1)
    meta[1:2, :] = jnp.broadcast_to(count, (1, TILE))
    for dx, core in line:
        send(meta, mbuf.at[g], ms_sem.at[0], m_sem.at[g], at(dx=dx, core=core))
    mbuf[g] = meta[...]
    gather_relay(0, RELAYS[:3])

    left, right, far_x = (x - 1) % X, (x + 1) % X, (x + 2) % X
    for q in range(2):
        for s, k, dx in ((left, q, 1), (right, 3 - q, -1)):
            ref = tile_chunk(s, k)
            send(ref, ref, as_sem.at[1], a_sem.at[s, k], at(dx=dx))
    gather_relay(0, RELAYS[3:])

    for s, ks in ((left, (2, 3)), (right, (1, 0)), (far_x, (0, 1, 2, 3))):
        for k in ks:
            tile_chunk(s, k)
        piece = a_all.at[s, rows(c)]
        send(piece, piece, as_sem.at[2], c_sem.at[s], sib)
    for dx, core in line:
        p = 2 * ((x + dx) % X) + core
        arrived(mbuf.at[p], m_sem.at[p])
    to_sm = [pltpu.make_async_copy(mbuf.at[2 * s, pl.ds(COLS_AT, SLOTS)], sm.at[s], l_sem.at[1 + s]) for s in range(X)]
    for copy in to_sm:
        copy.start()
    own_a.wait()
    for copy in to_sm:
        copy.wait()
    for h in range(HOPS):
        if h:
            gather_relay(h)
        arrived(a_all.at[h, rows(other)], c_sem.at[h])
        scale = prepare(h)
        gather_rest(h)
        compute(h, scale)

    for dx, core in line:
        p = 2 * ((x + dx) % X) + core
        arrived(obuf.at[p], o_sem.at[p])
    low = lax.broadcasted_iota(jnp.int32, (HALF, TILE), 1) < HALF
    for i in range(0, X, 2):
        p0, p1, q0, q1 = (obuf[2 * i + j].astype(jnp.float32) for j in range(4))
        turned = jnp.concatenate([p1[:, HALF:], p1[:, :HALF]], 1)
        at0 = CHIP * i
        out[:, at0:at0 + TILE] = jnp.where(low, p0, turned).astype(jnp.bfloat16)
        out[:, at0 + TILE:at0 + 2 * TILE] = jnp.where(low, turned, q0).astype(jnp.bfloat16)
        out[:, at0 + 2 * TILE:at0 + 3 * TILE] = q1.astype(jnp.bfloat16)

    arrived(half_x.at[pl.ds(0, WIDTH[other])], h_sem.at[0])
    arrived(a_all.at[0], as_sem.at[0])
    arrived(a_all.at[0, pl.ds(0, HALF)], as_sem.at[1])
    arrived(a_all.at[pl.ds(0, 2)], as_sem.at[2])
    arrived(mbuf.at[pl.ds(0, 7)], ms_sem.at[0])
    arrived(obuf.at[pl.ds(0, 7)], os_sem.at[0])
    for h in range(HOPS):
        arrived(xgs[h].at[pl.ds(0, 31), pl.ds(0, w)], s_sem.at[h])


def per_device(features, tile_cols, live_tiles, tile_values, degrees):
    a_in = tile_values[0].reshape(HALF, SLOTS * TILE)
    cols = jnp.swapaxes(tile_cols, 1, 2)
    vm = pl.BlockSpec(memory_space=pltpu.VMEM)
    dma = pltpu.SemaphoreType.DMA
    slab = pltpu.VMEM((BLOCKS, TILE, TILE), jnp.bfloat16)
    res = pl.pallas_call(
        kernel,
        out_shape=jax.ShapeDtypeStruct((HALF, X * CHIP), jnp.bfloat16),
        in_specs=[vm] * 5,
        out_specs=vm,
        scratch_shapes=[
            slab, slab, slab, slab,
            pltpu.VMEM((X, TILE, SLOTS * TILE), jnp.bfloat16),
            pltpu.VMEM((HOPS, TILE, TILE), jnp.bfloat16),
            pltpu.VMEM((HOPS, TILE, TILE), jnp.bfloat16),
            pltpu.VMEM((TILE, TILE), jnp.bfloat16),
            pltpu.VMEM((CHIP, TILE), jnp.bfloat16),
            pltpu.VMEM((24, TILE), jnp.int32),
            pltpu.VMEM((8, 24, TILE), jnp.int32),
            pltpu.VMEM((8, HALF, TILE), jnp.bfloat16),
            pltpu.VMEM((SLOTS * TILE, TILE), jnp.bfloat16),
            pltpu.SMEM((X, SLOTS, TILE), jnp.int32),
            dma((HOPS, BLOCKS)), dma((HOPS,)), dma((X, 4)), dma((X,)), dma((3,)),
            dma((8,)), dma((1,)), dma((8,)), dma((1,)), dma((2,)), dma((5,)),
        ],
        compiler_params=pltpu.CompilerParams(collective_id=0, has_side_effects=True, vmem_limit_bytes=40 * 1024 * 1024),
        name="propagate",
    )(features, cols, live_tiles, degrees, a_in)
    return res[None]


def solution(mesh):
    in_specs = (
        P("shard", None),
        P("section", None, None),
        P("section", None),
        P("section", "shard", None, None),
        P("section", "shard"),
    )
    return jax.shard_map(per_device, mesh=mesh, in_specs=in_specs,
                         out_specs=P("section", "shard", None), check_vma=False)
```

```python
import jax
import jax.numpy as jnp
from jax import lax
from jax.experimental import pallas as pl
from jax.experimental.pallas import tpu as pltpu
from jax.sharding import PartitionSpec as P

MESH = pl.DeviceIdType.MESH
X, Y, Z = 4, 4, 8
HOPS = 4
TILE = 128
SLOTS = 16
BLOCKS = Y * Z
HALF = 64
CHUNK = 16
CHIP = 192
WIDTH = (64, 128)
FIRST = (0, 64)
COLS_AT = 8
DYS = (0, 1, -1, 2)
DZS = (0, 1, -1, 2, -2, 3, -3, 4)


def parent(dy, dz):
    if dy == 0 or dz == 0:
        return (0, 0)
    if abs(dz) <= 2:
        return (dy, 0)
    return (0, dz)


def far(o):
    return abs(o[0]) + abs(o[1])


OFFSETS = [(dy, dz) for dz in DZS for dy in DYS if dy or dz]
KIDS = {}
for _o in sorted(OFFSETS, key=lambda o: -far(o)):
    KIDS.setdefault(parent(*_o), []).append(_o)
DIRECT = sorted(KIDS.pop((0, 0)), key=lambda o: (o not in KIDS, -far(o)))
RELAYS = sorted(KIDS, key=far)
LEAVES = [o for o in sorted(OFFSETS, key=lambda o: (far(o) + far(parent(*o)), far(o))) if o not in KIDS]


def send(src, dst, ssem, rsem, to):
    pltpu.make_async_remote_copy(src_ref=src, dst_ref=dst, send_sem=ssem, recv_sem=rsem,
                                 device_id=to, device_id_type=MESH).start()


def arrived(ref, sem):
    pltpu.make_async_copy(ref, ref, sem).wait()


def kernel(*refs):
    core = lax.axis_index("shard") % 2
    for c in (0, 1):
        @pl.when(core == c)
        def _():
            run(c, *refs)


def run(c, feat, cols, live, deg, a_in, out, xg0, xg1, xg2, xg3, a_all, ybuf, tbuf, half_x, ft, meta, mbuf, obuf, a_t, sm,
        r_sem, s_sem, a_sem, c_sem, as_sem, m_sem, ms_sem, o_sem, os_sem, h_sem, l_sem):
    x = lax.axis_index("section")
    sh = lax.axis_index("shard")
    z, y = sh // 8, (sh // 2) % 4
    g = 2 * x + c
    xgs = (xg0, xg1, xg2, xg3)
    other = 1 - c
    w = WIDTH[c]
    mine, theirs = pl.ds(FIRST[c], w), pl.ds(FIRST[other], WIDTH[other])

    def at(dx=0, dy=0, dz=0, core=c):
        return ((x + dx) % X, ((z + dz) % Z) * 8 + ((y + dy) % Y) * 2 + core)

    def blk(dy=0, dz=0):
        return ((y + dy) % Y) * Z + (z + dz) % Z

    def block(h, b):
        return xgs[h].at[b, pl.ds(0, w)]

    def rows(core, first=0, count=HALF):
        return pl.ds(core * HALF + first, count)

    line = [(dx, core) for dx in range(X) for core in (c, other) if (dx, core) != (0, c)]
    sib = at(core=other)

    barrier = pltpu.get_barrier_semaphore()
    peers = [at(dz=d) for d in (4, 3, 5, 2, 6, 1, 7)] + [at(dy=d) for d in (2, 1, 3)]
    peers += [at(dx=dx, core=core) for dx, core in line]
    for to in peers:
        pl.semaphore_signal(barrier, inc=1, device_id=to, device_id_type=MESH)

    for i in range(X):
        @pl.when(x == i)
        def _():
            part = feat[:, CHIP * i:CHIP * (i + 1)].astype(jnp.float32)
            none = jnp.zeros_like(part)
            ft[...] = jnp.concatenate([part, none] if c == 0 else [none, part], 0).T.astype(jnp.bfloat16)
    pl.semaphore_wait(barrier, len(peers))

    send(ft.at[theirs], half_x.at[pl.ds(0, WIDTH[other])], h_sem.at[0], h_sem.at[1], sib)

    for q in range(4):
        for dx, k in ((1, q), (-1, 3 - q)):
            send(a_in.at[pl.ds(k * CHUNK, CHUNK)], a_all.at[x, rows(c, k * CHUNK, CHUNK)],
                 as_sem.at[0], a_sem.at[x, k], at(dx=dx))
    send(a_in, a_all.at[x, rows(c)], as_sem.at[2], c_sem.at[x], sib)
    own_a = pltpu.make_async_copy(a_in, a_all.at[x, rows(c)], l_sem.at[0])
    own_a.start()

    def gather_start(h, src):
        b = blk()
        for dy, dz in DIRECT:
            send(src, block(h, b), s_sem.at[h], r_sem.at[h, b], at(dy=dy, dz=dz))

    def gather_relay(h, relays=RELAYS):
        for o in relays:
            b = blk(-o[0], -o[1])
            ref = block(h, b)
            arrived(ref, r_sem.at[h, b])
            for k in KIDS[o]:
                send(ref, ref, s_sem.at[h], r_sem.at[h, b], at(dy=k[0] - o[0], dz=k[1] - o[1]))

    def gather_rest(h):
        for o in LEAVES:
            b = blk(-o[0], -o[1])
            arrived(block(h, b), r_sem.at[h, b])

    def tile_chunk(s, k):
        ref = a_all.at[s, rows(c, k * CHUNK, CHUNK)]
        arrived(ref, a_sem.at[s, k])
        return ref

    def prepare(h):
        a_t[...] = a_all[h].T
        for k in range(SLOTS):
            on = (mbuf[2 * h, 1:2, :] > k).astype(jnp.float32).astype(jnp.bfloat16)
            a_t[k * TILE:(k + 1) * TILE, :] = a_t[k * TILE:(k + 1) * TILE, :] * on
        degree = mbuf[2 * h, 0:1, :] + mbuf[2 * h + 1, 0:1, :]
        return lax.rsqrt(degree.astype(jnp.float32))

    def compute(h, scale):
        acc = jnp.zeros((w, TILE), jnp.float32)
        for k in range(0, SLOTS, 4):
            src = jnp.concatenate([xgs[h][sm[h, k + i, 0], 0:w] for i in range(4)], axis=1)
            acc = acc + jnp.dot(src, a_t[k * TILE:(k + 4) * TILE, :], preferred_element_type=jnp.float32)
        val = acc * scale
        if h < HOPS - 1:
            ybuf[h, 0:w] = val.astype(jnp.bfloat16)
            xgs[h + 1][blk(), 0:w] = val.astype(jnp.bfloat16)
            gather_start(h + 1, ybuf.at[h, pl.ds(0, w)])
        wide = jnp.concatenate([val, val], 0) if w == HALF else val
        tbuf[h] = wide.T.astype(jnp.bfloat16)

        @pl.when(x == h)
        def _():
            obuf[g] = tbuf[h, c * HALF:(c + 1) * HALF]
            send(tbuf.at[h, rows(other)], obuf.at[g], os_sem.at[0], o_sem.at[g], sib)

        @pl.when(x != h)
        def _():
            for core in (0, 1):
                send(tbuf.at[h, rows(core)], obuf.at[g], os_sem.at[0], o_sem.at[g], (h, (sh // 2) * 2 + core))

    arrived(half_x.at[pl.ds(0, w)], h_sem.at[1])
    xg0[blk(), 0:w] = (ft[FIRST[c]:FIRST[c] + w].astype(jnp.float32) + half_x[0:w].astype(jnp.float32)).astype(jnp.bfloat16)
    gather_start(0, block(0, blk()))
    lane = lax.broadcasted_iota(jnp.int32, (SLOTS, BLOCKS), 1)
    col = jnp.sum(jnp.where(lane == sh // 2, cols[0], 0), axis=1, keepdims=True)
    col = (col & (Y - 1)) * Z + (col >> 2)
    meta[pl.ds(COLS_AT, SLOTS), :] = jnp.broadcast_to(col, (SLOTS, TILE))
    count = jnp.sum(jnp.where(lane[0:1] == sh // 2, live[...], 0), axis=1, keepdims=True)
    d = deg[...]
    none = jnp.zeros_like(d)
    meta[0:1, :] = jnp.concatenate([d, none] if c == 0 else [none, d], 1)
    meta[1:2, :] = jnp.broadcast_to(count, (1, TILE))
    for dx, core in line:
        send(meta, mbuf.at[g], ms_sem.at[0], m_sem.at[g], at(dx=dx, core=core))
    mbuf[g] = meta[...]
    gather_relay(0, RELAYS[:3])

    left, right, far_x = (x - 1) % X, (x + 1) % X, (x + 2) % X
    for q in range(2):
        for s, k, dx in ((left, q, 1), (right, 3 - q, -1)):
            ref = tile_chunk(s, k)
            send(ref, ref, as_sem.at[1], a_sem.at[s, k], at(dx=dx))
    gather_relay(0, RELAYS[3:])

    for s, ks in ((left, (2, 3)), (right, (1, 0)), (far_x, (0, 1, 2, 3))):
        for k in ks:
            tile_chunk(s, k)
        piece = a_all.at[s, rows(c)]
        send(piece, piece, as_sem.at[2], c_sem.at[s], sib)
    for dx, core in line:
        p = 2 * ((x + dx) % X) + core
        arrived(mbuf.at[p], m_sem.at[p])
    to_sm = [pltpu.make_async_copy(mbuf.at[2 * s, pl.ds(COLS_AT, SLOTS)], sm.at[s], l_sem.at[1 + s]) for s in range(X)]
    for copy in to_sm:
        copy.start()
    own_a.wait()
    for copy in to_sm:
        copy.wait()
    for h in range(HOPS):
        if h:
            gather_relay(h)
        arrived(a_all.at[h, rows(other)], c_sem.at[h])
        scale = prepare(h)
        gather_rest(h)
        compute(h, scale)

    for dx, core in line:
        p = 2 * ((x + dx) % X) + core
        arrived(obuf.at[p], o_sem.at[p])
    low = lax.broadcasted_iota(jnp.int32, (HALF, TILE), 1) < HALF
    for i in range(0, X, 2):
        p0, p1, q0, q1 = (obuf[2 * i + j].astype(jnp.float32) for j in range(4))
        turned = jnp.concatenate([p1[:, HALF:], p1[:, :HALF]], 1)
        at0 = CHIP * i
        out[:, at0:at0 + TILE] = jnp.where(low, p0, turned).astype(jnp.bfloat16)
        out[:, at0 + TILE:at0 + 2 * TILE] = jnp.where(low, turned, q0).astype(jnp.bfloat16)
        out[:, at0 + 2 * TILE:at0 + 3 * TILE] = q1.astype(jnp.bfloat16)

    arrived(half_x.at[pl.ds(0, WIDTH[other])], h_sem.at[0])
    arrived(a_all.at[0], as_sem.at[0])
    arrived(a_all.at[0, pl.ds(0, HALF)], as_sem.at[1])
    arrived(a_all.at[pl.ds(0, 2)], as_sem.at[2])
    arrived(mbuf.at[pl.ds(0, 7)], ms_sem.at[0])
    arrived(obuf.at[pl.ds(0, 7)], os_sem.at[0])
    for h in range(HOPS):
        arrived(xgs[h].at[pl.ds(0, 31), pl.ds(0, w)], s_sem.at[h])


def per_device(features, tile_cols, live_tiles, tile_values, degrees):
    a_in = tile_values[0].reshape(HALF, SLOTS * TILE)
    cols = jnp.swapaxes(tile_cols, 1, 2)
    vm = pl.BlockSpec(memory_space=pltpu.VMEM)
    dma = pltpu.SemaphoreType.DMA
    slab = pltpu.VMEM((BLOCKS, TILE, TILE), jnp.bfloat16)
    res = pl.pallas_call(
        kernel,
        out_shape=jax.ShapeDtypeStruct((HALF, X * CHIP), jnp.bfloat16),
        in_specs=[vm] * 5,
        out_specs=vm,
        scratch_shapes=[
            slab, slab, slab, slab,
            pltpu.VMEM((X, TILE, SLOTS * TILE), jnp.bfloat16),
            pltpu.VMEM((HOPS, TILE, TILE), jnp.bfloat16),
            pltpu.VMEM((HOPS, TILE, TILE), jnp.bfloat16),
            pltpu.VMEM((TILE, TILE), jnp.bfloat16),
            pltpu.VMEM((CHIP, TILE), jnp.bfloat16),
            pltpu.VMEM((24, TILE), jnp.int32),
            pltpu.VMEM((8, 24, TILE), jnp.int32),
            pltpu.VMEM((8, HALF, TILE), jnp.bfloat16),
            pltpu.VMEM((SLOTS * TILE, TILE), jnp.bfloat16),
            pltpu.SMEM((X, SLOTS, TILE), jnp.int32),
            dma((HOPS, BLOCKS)), dma((HOPS,)), dma((X, 4)), dma((X,)), dma((3,)),
            dma((8,)), dma((1,)), dma((8,)), dma((1,)), dma((2,)), dma((5,)),
        ],
        compiler_params=pltpu.CompilerParams(collective_id=0, has_side_effects=True, vmem_limit_bytes=40 * 1024 * 1024),
        name="propagate",
    )(features, cols, live_tiles, degrees, a_in)
    return res[None]


def solution(mesh):
    in_specs = (
        P("shard", None),
        P("section", None, None),
        P("section", None),
        P("section", "shard", None, None),
        P("section", "shard"),
    )
    return jax.shard_map(per_device, mesh=mesh, in_specs=in_specs,
                         out_specs=P("section", "shard", None), check_vma=False)
```
